128 devices in a mesh: row: 8 (over y, core), col: 16 (over z, x).
Axes of the slice: x: 4, y: 4, z: 4, core: 2. Of those that a mesh axis runs over, the one named last changes fastest.
Arguments:
- weight: bfloat16 [8192, 16384], P('row', 'col'), may hold values from -3 to 3
- momentum: float32 [8192, 16384], P('row', 'col'), may hold values from -100 to 100, as said below
- gradient: bfloat16 [8192, 16384], P('row', 'col'), may hold values from -6 to 6
- prev_basis: bfloat16 [16384, 512], P('col'), may hold values from -6 to 6
Outputs:
- new_weight: bfloat16 [8192, 16384], P('row', 'col')
- new_momentum: float32 [8192, 16384], P('row', 'col')
- new_basis: bfloat16 [16384, 512], P('col')
The draws below stay inside these ranges and needn't reach their ends.
Inputs may be any that keep to these rules, and one draw needn't show every extreme that they name: momentum has rows and columns of different scales.
All inputs are finite; a program needn't handle non-finite values.
Results may differ from the reference program's by a relative error of at most 0.0021.
Values may be sent and summed in bfloat16 or wider, within the bound.
A program may use at most 128 MiB of HBM per device.

```python
import jax
import jax.numpy as jnp
from jax import lax

M = 8192
N = 16384
R = 512
COLS_DEV = 1024


def draw_momentum(key, part):
    row_key = jax.random.fold_in(key, 11)
    col_key = jax.random.fold_in(key, 12)
    entry_key = jax.random.fold_in(key, 13)
    positions = jnp.arange(N, dtype=jnp.float32) / N
    inside = (jnp.arange(N, dtype=jnp.int32) % COLS_DEV).astype(jnp.float32) / COLS_DEV
    spread = jax.random.uniform(col_key, (N,), jnp.float32)
    row_scale = 10.0 ** jax.random.uniform(row_key, (M, 1), jnp.float32)
    col_power = 0.3 * spread + 0.3 * positions + 0.5 * inside
    entries = jnp.clip(jax.random.normal(entry_key, (M, N), jnp.float32), -6.0, 6.0)
    col_scale = (10.0 ** col_power)[None, :]
    return entries * row_scale * col_scale / 20.0


def block_levels(key, extent, cuts, smallest, top_value):
    level = 1.0
    for position, blocks in cuts:
        draws = jax.random.uniform(jax.random.fold_in(jax.random.fold_in(key, 6), position), (blocks,), jnp.float32, smallest / len(cuts), top_value / len(cuts))
        level = level * jnp.repeat(jnp.exp(draws), extent[position] // blocks).reshape((-1,) + (1,) * (len(extent) - 1 - position))
    return level


def scatter_about(stream_key, extent, deviation, limit, split=(), kind=jnp.bfloat16):
    factor_of = block_levels(stream_key, extent, split, -0.22, 0.18) if split else 1.0
    drawn = jax.random.normal(stream_key, extent, jnp.float32) * deviation * factor_of
    return jnp.minimum(jnp.maximum(drawn, -limit), limit).astype(kind)


def setup_inputs(seed: int = 0) -> dict:
    splits = jax.random.split(jax.random.key(seed), 5)
    weight = scatter_about(splits[0], (M, N), 0.5, 3.0, ((0, 8), (1, 16)))
    momentum = draw_momentum(jax.random.fold_in(splits[4], 71), 0)
    gradient = scatter_about(splits[2], (M, N), 1.0, 6.0, ((0, 8), (1, 16)))
    prev_basis = scatter_about(splits[3], (N, R), 1.0, 6.0, ((0, 16),))
    return {"weight": weight, "momentum": momentum, "gradient": gradient, "prev_basis": prev_basis}


decay_loss = 0.1
step_size = 0.4
epsilon = 1e-06

def reference(weight, momentum, gradient, prev_basis):
    high = lax.Precision.HIGHEST
    buffer = momentum + gradient.astype(jnp.float32)
    left_factor = jnp.dot(buffer, prev_basis.astype(jnp.float32), precision=high)
    gram_matrix = jnp.dot(left_factor.T, left_factor, precision=high)
    lower_tri = jnp.linalg.cholesky(gram_matrix)
    orthonormal = jax.scipy.linalg.solve_triangular(lower_tri, left_factor.T, lower=True).T
    right_factor = jnp.dot(buffer.T, orthonormal, precision=high)
    column_scale = jnp.sqrt(lax.optimization_barrier(jnp.sum(right_factor * right_factor, axis=0)) / N + epsilon)
    new_basis = (right_factor / column_scale).astype(jnp.bfloat16)
    basis_float = new_basis.astype(jnp.float32)
    new_momentum = buffer - decay_loss * jnp.dot(orthonormal * column_scale, basis_float.T, precision=high)
    update = jnp.dot(orthonormal, basis_float.T, precision=high)
    new_weight = (weight.astype(jnp.float32) - step_size * (M / N) ** 0.5 * update).astype(jnp.bfloat16)
    return (new_weight, new_momentum, new_basis)
```

```python
import functools

import jax
import jax.numpy as jnp
from jax import lax
from jax.experimental import pallas as pl
from jax.experimental.pallas import tpu as pltpu
from jax.sharding import PartitionSpec as P

MESH = pl.DeviceIdType.MESH
F32 = jnp.float32
BF16 = jnp.bfloat16

M = 8192
N = 16384
R = 512
ROWS = 1024
COLS = 1024
NB = 128
SLICE = 128
SUB = 32

decay_loss = 0.1
step_size = 0.4
epsilon = 1e-06


def dims(a, b):
    return (((a,), (b,)), ((), ()))


def dot(a, b):
    return jnp.dot(a, b, preferred_element_type=F32)


def dot_t(a, b):
    return lax.dot_general(a, b, dims(0, 0), preferred_element_type=F32)


def dot_nt(a, b):
    return lax.dot_general(a, b, dims(1, 1), preferred_element_type=F32)


def split(x):
    high = x.astype(BF16)
    return high, (x - high.astype(F32)).astype(BF16)


def from_row(x, i):
    return jnp.broadcast_to(x[i : i + 1, :], x.shape)


def from_lane(x, k):
    return jnp.broadcast_to(x[:, k : k + 1], (8, NB))


HALF = NB // 16


def exact(a, b, contract):
    return lax.dot_general(
        a, b, contract, precision=lax.Precision.HIGHEST, preferred_element_type=F32
    )


def invert_leaf(z_ref):
    rows = lax.broadcasted_iota(jnp.int32, (8, NB), 0)
    lanes = lax.broadcasted_iota(jnp.int32, (8, NB), 1)
    tiles = [z_ref[8 * i : 8 * i + 8, :] for i in range(NB // 8)]
    for p in range(NB // 8):
        tile = tiles[p]
        columns = [from_lane(tile, 8 * p + k) for k in range(8)]
        own = (lanes >= 8 * p) & (lanes < 8 * p + 8)
        tile = jnp.where(own, jnp.where(lanes - 8 * p == rows, 1.0, 0.0), tile)
        below = tiles[p + 1 : (p // HALF + 1) * HALF]
        near = [from_lane(below[0], 8 * p + k) for k in range(8)] if below else None
        upper, factors = [], []
        for j in range(8):
            inverse = lax.rsqrt(from_row(columns[j], j))
            t = columns[j] * inverse
            masked = jnp.where(rows > j, t, 0.0)
            u = from_row(tile, j) * inverse
            upper.append(u)
            tile = jnp.where(rows == j, u, tile - masked * u)
            if near:
                factors.append(near[j] * inverse)
            for k in range(j + 1, 8):
                tk = from_row(t, k)
                columns[k] = columns[k] - masked * tk
                if near:
                    near[k] = near[k] - factors[j] * tk
        tiles[p] = tile

        def eliminated(x, factors):
            terms = [t * u for t, u in zip(factors, upper)]
            while len(terms) > 1:
                terms = [terms[i] + terms[i + 1] for i in range(0, len(terms), 2)]
            return jnp.where(own, 0.0, x) - terms[0]

        if below:
            tiles[p + 1] = eliminated(below[0], factors)
        if len(below) > 1:
            turned = tile.T
            for i in range(p + 2, p + 1 + len(below)):
                part = turned[8 * i : 8 * i + 8, :]
                tiles[i] = eliminated(tiles[i], [from_lane(part, k) for k in range(8)])
        if p == HALF - 1:
            done = jnp.concatenate(tiles[:HALF], axis=0)
            row = lax.broadcasted_iota(jnp.int32, done.shape, 0)
            lane = lax.broadcasted_iota(jnp.int32, done.shape, 1)
            inside = lane < 8 * HALF
            rest = jnp.concatenate(tiles[HALF:], axis=0)
            rest = jnp.where(inside, 0.0, rest) - exact(
                done[:, 8 * HALF :], jnp.where(inside & (lane > row), 0.0, done), dims(0, 0)
            )
            tiles[HALF:] = [rest[8 * i : 8 * i + 8, :] for i in range(HALF)]
    for i in range(NB // 8):
        z_ref[8 * i : 8 * i + 8, :] = tiles[i]


def invert_cholesky(z_ref, d_ref, between):
    lower = lax.broadcasted_iota(jnp.int32, (NB, NB), 0) >= lax.broadcasted_iota(
        jnp.int32, (NB, NB), 1
    )
    for b in range(R // NB):
        lo, hi = b * NB, (b + 1) * NB
        d_ref[...] = z_ref[lo:hi, lo:hi]
        invert_leaf(d_ref)
        block = jnp.where(lower, d_ref[...], 0.0)
        z_ref[lo:hi, lo:hi] = block
        if b:
            z_ref[lo:hi, :lo] = exact(block, z_ref[lo:hi, :lo], dims(1, 0))
        if hi < R:
            upper = exact(block, z_ref[lo:hi, hi:], dims(1, 0))
            z_ref[lo:hi, hi:] = upper
            z_ref[hi:, lo:hi] = jnp.zeros((R - hi, NB), F32)
            z_ref[hi:, :] -= exact(upper, z_ref[lo:hi, :], dims(0, 0))
            z_ref[lo:hi, hi:] = jnp.zeros((NB, R - hi), F32)
        between(b)


class Copies:
    def __init__(self, send_sems, recv_sems):
        self.send_sems, self.recv_sems = send_sems, recv_sems
        self.count = 0
        self.unfinished = []

    def start(self, src, dst, device):
        i = self.count
        self.count += 1
        copy = pltpu.make_async_remote_copy(
            src_ref=src,
            dst_ref=dst,
            send_sem=self.send_sems.at[i],
            recv_sem=self.recv_sems.at[i],
            device_id=device,
            device_id_type=MESH,
        )
        copy.start()
        self.unfinished.append(copy)
        return copy

    def finish(self):
        for copy in self.unfinished:
            copy.wait_send()


class Ring:
    def __init__(self, copies, place, right, left, columns=slice(None)):
        self.copies, self.place, self.right, self.left = copies, place, right, left
        self.columns = columns

    def rows(self, base, size, ahead, part=None):
        start = base + size * lax.rem(self.place + ahead, 4)
        if part is None:
            return pl.ds(pl.multiple_of(start, 8), size)
        return pl.ds(pl.multiple_of(start + part * (size // 2), 8), size // 2)

    def scatter_far(self, src, base, size, far, near):
        self.src, self.base, self.size, self.far, self.near = src, base, size, far, near
        start, cols = self.copies.start, self.columns
        self.far_right = start(
            src.at[self.rows(base, size, 2, 0), cols], far.at[0, :, cols], self.right
        )
        self.far_left = start(
            src.at[self.rows(base, size, 2, 1), cols], far.at[1, :, cols], self.left
        )

    def scatter_near(self):
        src, base, size, near, cols = self.src, self.base, self.size, self.near, self.columns
        half = size // 2
        self.near_right = self.copies.start(
            src.at[self.rows(base, size, 1, 1), cols], near.at[0, half:, cols], self.right
        )
        self.near_left = self.copies.start(
            src.at[self.rows(base, size, 3, 0), cols], near.at[1, :half, cols], self.left
        )

    def scatter_start(self, *args):
        self.scatter_far(*args)
        self.scatter_near()

    def scatter_middle(self):
        half, cols = self.size // 2, self.columns
        self.far_right.wait_recv()
        rows = self.rows(self.base, self.size, 1, 0)
        self.src[rows, cols] += self.far[0, :, cols]
        self.last_right = self.copies.start(
            self.src.at[rows, cols], self.near.at[0, :half, cols], self.right
        )
        self.far_left.wait_recv()
        rows = self.rows(self.base, self.size, 3, 1)
        self.src[rows, cols] += self.far[1, :, cols]
        self.last_left = self.copies.start(
            self.src.at[rows, cols], self.near.at[1, half:, cols], self.left
        )

    def scatter_end(self, out, out_rows):
        cols = self.columns
        for copy in (self.near_right, self.near_left, self.last_right, self.last_left):
            copy.wait_recv()
        own = self.src[self.rows(self.base, self.size, 0), cols]
        out[out_rows, cols] = own + self.near[0, :, cols] + self.near[1, :, cols]

    def gather_start(self, buf, base, size):
        self.buf, self.base, self.size = buf, base, size
        own = buf.at[self.rows(base, size, 0), self.columns]
        self.to_right = self.copies.start(own, own, self.right)
        self.to_left = self.copies.start(own, own, self.left)

    def gather_middle(self):
        self.to_right.wait_recv()
        part = self.buf.at[self.rows(self.base, self.size, 3, 0), self.columns]
        self.on_right = self.copies.start(part, part, self.right)
        self.to_left.wait_recv()
        part = self.buf.at[self.rows(self.base, self.size, 1, 1), self.columns]
        self.on_left = self.copies.start(part, part, self.left)

    def gather_end(self):
        self.on_right.wait_recv()
        self.on_left.wait_recv()


BLOCKS = [(i, j) for i in range(R // NB) for j in range(i, R // NB)]
PACKED = len(BLOCKS) * NB
LIMIT = 42 * 1024 * 1024
COPIES = 128
CHUNKS = [slice(0, R // 2), slice(R // 2, R)]


def kernel(
    momentum, gradient, weight, basis,
    right_out, scaled_out, high_out, low_out, buffer_out, weight_out,
    mom, grad, prev, high, low, high_t, low_t,
    part, first_a, first_b, left, far_x, near_x, far_z, near_z, far_x2, near_x2, far_z2, near_z2,
    gram, packed, packed_in, packed_sum, gram_far, gram_near,
    right, right_in, right_sum, right_far, right_near,
    tri, block, tri_h, tri_l, squares,
    load_sems, send_sems, recv_sems,
):
    r, c = lax.axis_index("row"), lax.axis_index("col")
    y, core = r // 2, lax.rem(r, 2)
    z, x = c // 4, lax.rem(c, 4)

    def at(dy=0, dz=0, dx=0):
        return (
            lax.rem(y + dy, 4) * 2 + core,
            lax.rem(z + dz, 4) * 4 + lax.rem(x + dx, 4),
        )

    sibling = (y * 2 + 1 - core, c)

    order = []
    for ahead in (2, 1, 3, 0):
        order.append(lax.rem(x + ahead, 4) * SLICE)
        order.append(ROWS // 2 + lax.rem(z + ahead, 4) * SLICE)
    order = [pl.ds(pl.multiple_of(start, SLICE), SLICE) for start in order]
    load_basis = pltpu.make_async_copy(basis, prev, load_sems.at[16])
    load_basis.start()
    loads = []
    for i, rows in enumerate(order):
        a = pltpu.make_async_copy(momentum.at[rows], mom.at[rows], load_sems.at[2 * i])
        b = pltpu.make_async_copy(gradient.at[rows], grad.at[rows], load_sems.at[2 * i + 1])
        a.start()
        b.start()
        loads.append((a, b))

    barrier = pltpu.get_barrier_semaphore()
    peers = [sibling, at(dy=1), at(dy=3)] + [(r, lax.rem(c + k, 16)) for k in range(1, 16)]
    for peer in peers:
        pl.semaphore_signal(barrier, inc=1, device_id=peer, device_id_type=MESH)

    copies = Copies(send_sems, recv_sems)
    x_ring = lambda cols: Ring(copies, x, at(dx=1), at(dx=3), cols)
    z_ring = lambda cols: Ring(copies, z, at(dz=1), at(dz=3), cols)
    outer = [(x_ring(cols), z_ring(cols)) for cols in CHUNKS]
    inner = [(z_ring(cols), x_ring(cols)) for cols in CHUNKS]
    ring_g = Ring(copies, y, at(dy=1), at(dy=3))
    ring_w = Ring(copies, y, at(dy=1), at(dy=3))

    def partial_left(i):
        rows = order[i]
        for load in loads[i]:
            load.wait()
        buffer = mom[rows, :] + grad[rows, :].astype(F32)
        buffer_out[rows, :] = buffer
        h, l = split(buffer)
        high[rows, :] = h
        low[rows, :] = l
        both = dot(jnp.concatenate([h, l], axis=0), prev[...])
        part[rows, :] = both[:SLICE] + both[SLICE:]

    load_basis.wait()
    for i in range(2):
        partial_left(i)
    pl.semaphore_wait(barrier, len(peers))
    for a, b in outer:
        a.scatter_far(part, 0, SLICE, far_x, near_x)
        b.scatter_far(part, ROWS // 2, SLICE, far_z, near_z)
    for i in range(2, 6):
        partial_left(i)
    for a, b in outer:
        a.scatter_near()
        b.scatter_near()
    for i in range(6, 8):
        partial_left(i)
    for a, b in outer:
        a.scatter_middle()
        b.scatter_middle()

    load_weight = pltpu.make_async_copy(weight, weight_out, load_sems.at[17])
    load_weight.start()

    @pl.loop(0, ROWS // NB)
    def _(k):
        rows = pl.ds(pl.multiple_of(k * NB, NB), NB)
        high_t[:, rows] = high[rows, :].T
        low_t[:, rows] = low[rows, :].T

    everything = pl.ds(0, SLICE)
    for (a, b), (a2, b2) in zip(outer, inner):
        a.scatter_end(first_a, everything)
        a2.scatter_start(first_a, 0, SUB, far_z2, near_z2)
        b.scatter_end(first_b, everything)
        b2.scatter_start(first_b, 0, SUB, far_x2, near_x2)
    for a2, b2 in inner:
        a2.scatter_middle()
        b2.scatter_middle()
    base_a = x * SLICE
    base_b = ROWS // 2 + z * SLICE
    for a2, b2 in inner:
        a2.scatter_end(left, a2.rows(base_a, SUB, 0))
        a2.gather_start(left, base_a, SUB)
        b2.scatter_end(left, b2.rows(base_b, SUB, 0))
        b2.gather_start(left, base_b, SUB)
    for a2, b2 in inner:
        a2.gather_middle()
        b2.gather_middle()
    for (a, b), (a2, b2) in zip(outer, inner):
        a2.gather_end()
        a.gather_start(left, 0, SLICE)
        b2.gather_end()
        b.gather_start(left, ROWS // 2, SLICE)

    def slices(ahead):
        return (
            pl.ds(pl.multiple_of(lax.rem(x + ahead, 4) * SLICE, SLICE), SLICE),
            pl.ds(pl.multiple_of(ROWS // 2 + lax.rem(z + ahead, 4) * SLICE, SLICE), SLICE),
        )

    def halves(ahead):
        a, b = slices(ahead)
        return split(jnp.concatenate([left[a, :], left[b, :]], axis=0))

    def add_gram(ahead, first):
        h, l = halves(ahead)
        for i in range(R // NB):
            lo, hi = i * NB, (i + 1) * NB
            hl, ll = h[:, lo:hi], l[:, lo:hi]
            term = dot_t(hl, h[:, lo:]) + (
                dot_t(hl, l[:, lo:]) + dot_t(ll, h[:, lo:]) + dot_t(ll, l[:, lo:])
            )
            if first:
                gram[lo:hi, lo:] = term
            else:
                gram[lo:hi, lo:] += term

    def add_right(ahead, first):
        a, b = slices(ahead)
        h, l = halves(ahead)

        @pl.loop(0, COLS // 256)
        def _(k):
            rows = pl.ds(pl.multiple_of(k * 256, 256), 256)
            bh = jnp.concatenate([high_t[rows, a], high_t[rows, b]], axis=1)
            bl = jnp.concatenate([low_t[rows, a], low_t[rows, b]], axis=1)
            both = dot(jnp.concatenate([bh, bl], axis=0), h)
            term = both[:256] + (dot(bh, l) + both[256:])
            if first:
                right[rows, :] = term
            else:
                right[rows, :] += term

    add_gram(0, True)
    add_right(0, True)
    for a, b in outer:
        a.gather_middle()
        b.gather_middle()
    add_gram(1, False)
    add_gram(3, False)
    add_right(1, False)
    add_right(3, False)
    for a, b in outer:
        a.gather_end()
        b.gather_end()
    add_gram(2, False)

    for k, (i, j) in enumerate(BLOCKS):
        packed[k * NB : (k + 1) * NB, :] = gram[i * NB : (i + 1) * NB, j * NB : (j + 1) * NB]

    def half_of(whole, which):
        return pl.ds(pl.multiple_of(which * (whole // 2), 8), whole // 2)

    mine_g, other_g = half_of(PACKED, core), half_of(PACKED, 1 - core)
    mine_w, other_w = half_of(COLS, core), half_of(COLS, 1 - core)
    swap_g = copies.start(packed.at[other_g], packed_in, sibling)
    add_right(2, False)
    swap_w = copies.start(right.at[other_w], right_in, sibling)
    swap_g.wait_recv()
    packed[mine_g, :] += packed_in[...]
    ring_g.scatter_start(packed, core * (PACKED // 2), PACKED // 8, gram_far, gram_near)
    ring_g.scatter_middle()
    swap_w.wait_recv()
    right[mine_w, :] += right_in[...]
    ring_w.scatter_far(right, core * (COLS // 2), COLS // 8, right_far, right_near)
    ring_g.scatter_end(packed_sum, ring_g.rows(core * (PACKED // 2), PACKED // 8, 0))
    ring_g.gather_start(packed_sum, core * (PACKED // 2), PACKED // 8)
    ring_w.scatter_near()
    ring_g.gather_middle()
    ring_g.gather_end()
    back_g = copies.start(packed_sum.at[mine_g], packed_sum.at[mine_g], sibling)
    ring_w.scatter_middle()
    back_g.wait_recv()
    for k, (i, j) in enumerate(BLOCKS):
        tri[i * NB : (i + 1) * NB, j * NB : (j + 1) * NB] = packed_sum[k * NB : (k + 1) * NB, :]

    swaps = []

    def between(b):
        if b == 0:
            ring_w.scatter_end(right_sum, ring_w.rows(core * (COLS // 2), COLS // 8, 0))
            ring_w.gather_start(right_sum, core * (COLS // 2), COLS // 8)
        elif b == 1:
            ring_w.gather_middle()
        elif b == 2:
            ring_w.gather_end()
            swaps.append(
                copies.start(right_sum.at[mine_w], right_sum.at[mine_w], sibling)
            )

    invert_cholesky(tri, block, between)
    swaps[0].wait_recv()

    tri_h[...], tri_l[...] = split(tri[...].T)
    squares[c] = jnp.zeros((8, R), F32)
    h2 = R // 2

    def solved(value):
        h, l = split(value)
        n = len(value)
        both = jnp.concatenate([h, l], axis=0)
        halves = []
        for width, out in ((h2, slice(0, h2)), (R, slice(h2, R))):
            p = dot(both[:, :width], tri_h[:width, out])
            q = dot(h[:, :width], tri_l[:width, out])
            halves.append(p[:n] + (p[n:] + q))
        return jnp.concatenate(halves, axis=1)

    @pl.loop(0, COLS // 256)
    def _(k):
        rows = pl.ds(pl.multiple_of(k * 256, 256), 256)
        value = solved(right_sum[rows, :])
        mom[rows, R:] = value
        squares[c] += jnp.sum((value * value).reshape(32, 8, R), axis=0)

    sums = []
    for k in range(1, 16):
        sums.append(copies.start(squares.at[c], squares.at[c], (r, lax.rem(c + k, 16))))

    @pl.loop(0, ROWS // 256)
    def _(k):
        rows = pl.ds(pl.multiple_of(k * 256, 256), 256)
        value = solved(left[rows, :])
        mom[rows, :R] = value
        h, l = split(value)
        high_out[rows, :] = h
        low_out[rows, :] = l

    for copy in sums:
        copy.wait_recv()
    total = squares[0]
    for k in range(1, 16):
        total = total + squares[k]
    total = jnp.sum(total, axis=0, keepdims=True)
    scale = jnp.sqrt(total / N + epsilon)
    inverse = 1.0 / scale
    right_out[...] = (mom[:, R:] * inverse).astype(BF16)
    scaled_out[...] = (mom[:, :R] * scale).astype(BF16)
    load_weight.wait()
    copies.finish()


def factors(momentum, gradient, weight, basis):
    vmem = pl.BlockSpec(memory_space=pltpu.VMEM)
    any_ = pl.BlockSpec(memory_space=pltpu.HBM)
    f = lambda *s: pltpu.VMEM(s, F32)
    b = lambda *s: pltpu.VMEM(s, BF16)
    ring = lambda s, w: [f(2, s // 2, w), f(2, s, w)]
    return pl.pallas_call(
        kernel,
        out_shape=[
            jax.ShapeDtypeStruct((COLS, R), BF16),
            jax.ShapeDtypeStruct((ROWS, R), BF16),
            jax.ShapeDtypeStruct((ROWS, R), BF16),
            jax.ShapeDtypeStruct((ROWS, R), BF16),
            jax.ShapeDtypeStruct((ROWS, COLS), F32),
            jax.ShapeDtypeStruct((ROWS, COLS), BF16),
        ],
        in_specs=[any_] * 4,
        out_specs=[vmem] * 6,
        scratch_shapes=[
            f(ROWS, COLS), b(ROWS, COLS), b(COLS, R),
            b(ROWS, COLS), b(ROWS, COLS), b(COLS, ROWS), b(COLS, ROWS),
            f(ROWS, R), f(SLICE, R), f(SLICE, R), f(ROWS, R),
            *ring(SLICE, R), *ring(SLICE, R), *ring(SUB, R), *ring(SUB, R),
            f(R, R), f(PACKED, NB), f(PACKED // 2, NB), f(PACKED, NB), *ring(PACKED // 8, NB),
            f(COLS, R), f(COLS // 2, R), f(COLS, R), *ring(COLS // 8, R),
            f(R, R), f(NB, NB), b(R, R), b(R, R), f(16, 8, R),
            pltpu.SemaphoreType.DMA((18,)),
            pltpu.SemaphoreType.DMA((COPIES,)),
            pltpu.SemaphoreType.DMA((COPIES,)),
        ],
        compiler_params=pltpu.CompilerParams(
            collective_id=0, has_side_effects=True, vmem_limit_bytes=LIMIT
        ),
        name="factors",
    )(momentum, gradient, weight, basis)


def last_kernel(b, w, scaled, high, low, v, basis, new_w, new_m, new_v):
    buffer = b[...]
    vs = v[...]
    rows = len(buffer)
    both = dot_nt(jnp.concatenate([scaled[...], high[...], low[...]], axis=0), vs)
    new_m[...] = buffer - decay_loss * both[:rows]
    update = both[rows : 2 * rows] + both[2 * rows :]
    rate = step_size * (M / N) ** 0.5
    new_w[...] = (w[...].astype(F32) - rate * update).astype(BF16)
    new_v[...] = basis[...]


def outputs(buffer, weight, scaled, high, low, v):
    rows = 256
    wide = pl.BlockSpec((rows, COLS), lambda i: (i, 0))
    thin = pl.BlockSpec((rows, R), lambda i: (i, 0))
    whole = pl.BlockSpec((COLS, R), lambda i: (0, 0))
    return pl.pallas_call(
        last_kernel,
        grid=(ROWS // rows,),
        out_shape=[
            jax.ShapeDtypeStruct((ROWS, COLS), BF16),
            jax.ShapeDtypeStruct((ROWS, COLS), F32),
            jax.ShapeDtypeStruct((COLS, R), BF16),
        ],
        in_specs=[wide, wide, thin, thin, thin, whole, thin],
        out_specs=[wide, wide, thin],
        compiler_params=pltpu.CompilerParams(vmem_limit_bytes=20 * 1024 * 1024),
        name="outputs",
    )(buffer, weight, scaled, high, low, v, v)


def per_device(weight, momentum, gradient, prev_basis):
    kept = [
        pltpu.with_memory_space_constraint(a, pltpu.HBM)
        for a in (momentum, gradient, weight, prev_basis)
    ]
    v, *rest, buffer, held = factors(*kept)
    return tuple(outputs(buffer, held, *rest, v))


def solution(mesh):
    return jax.shard_map(
        per_device,
        mesh=mesh,
        in_specs=(P("row", "col"), P("row", "col"), P("row", "col"), P("col", None)),
        out_specs=(P("row", "col"), P("row", "col"), P("col", None)),
        check_vma=False,
    )
```

```python
import functools

import jax
import jax.numpy as jnp
from jax import lax
from jax.experimental import pallas as pl
from jax.experimental.pallas import tpu as pltpu
from jax.sharding import PartitionSpec as P

MESH = pl.DeviceIdType.MESH
F32 = jnp.float32
BF16 = jnp.bfloat16

M = 8192
N = 16384
R = 512
ROWS = 1024
COLS = 1024
NB = 128
SLICE = 128
SUB = 32

decay_loss = 0.1
step_size = 0.4
epsilon = 1e-06


def dims(a, b):
    return (((a,), (b,)), ((), ()))


def dot(a, b):
    return jnp.dot(a, b, preferred_element_type=F32)


def dot_t(a, b):
    return lax.dot_general(a, b, dims(0, 0), preferred_element_type=F32)


def dot_nt(a, b):
    return lax.dot_general(a, b, dims(1, 1), preferred_element_type=F32)


def split(x):
    high = x.astype(BF16)
    return high, (x - high.astype(F32)).astype(BF16)


def from_row(x, i):
    return jnp.broadcast_to(x[i : i + 1, :], x.shape)


def from_lane(x, k):
    return jnp.broadcast_to(x[:, k : k + 1], (8, NB))


HALF = NB // 16


def exact(a, b, contract):
    return lax.dot_general(
        a, b, contract, precision=lax.Precision.HIGHEST, preferred_element_type=F32
    )


def invert_leaf(z_ref, between):
    rows = lax.broadcasted_iota(jnp.int32, (8, NB), 0)
    lanes = lax.broadcasted_iota(jnp.int32, (8, NB), 1)
    tiles = [z_ref[8 * i : 8 * i + 8, :] for i in range(NB // 8)]
    for p in range(NB // 8):
        tile = tiles[p]
        columns = [from_lane(tile, 8 * p + k) for k in range(8)]
        own = (lanes >= 8 * p) & (lanes < 8 * p + 8)
        tile = jnp.where(own, jnp.where(lanes - 8 * p == rows, 1.0, 0.0), tile)
        below = tiles[p + 1 : (p // HALF + 1) * HALF]
        near = [from_lane(below[0], 8 * p + k) for k in range(8)] if below else None
        upper, factors = [], []
        for j in range(8):
            inverse = lax.rsqrt(from_row(columns[j], j))
            t = columns[j] * inverse
            masked = jnp.where(rows > j, t, 0.0)
            u = from_row(tile, j) * inverse
            upper.append(u)
            tile = jnp.where(rows == j, u, tile - masked * u)
            if near:
                factors.append(near[j] * inverse)
            for k in range(j + 1, 8):
                tk = from_row(t, k)
                columns[k] = columns[k] - masked * tk
                if near:
                    near[k] = near[k] - factors[j] * tk
        tiles[p] = tile

        def eliminated(x, factors):
            terms = [t * u for t, u in zip(factors, upper)]
            while len(terms) > 1:
                terms = [terms[i] + terms[i + 1] for i in range(0, len(terms), 2)]
            return jnp.where(own, 0.0, x) - terms[0]

        if below:
            tiles[p + 1] = eliminated(below[0], factors)
        if len(below) > 1:
            turned = tile.T
            for i in range(p + 2, p + 1 + len(below)):
                part = turned[8 * i : 8 * i + 8, :]
                tiles[i] = eliminated(tiles[i], [from_lane(part, k) for k in range(8)])
        if p == HALF - 1:
            between()
            done = jnp.concatenate(tiles[:HALF], axis=0)
            row = lax.broadcasted_iota(jnp.int32, done.shape, 0)
            lane = lax.broadcasted_iota(jnp.int32, done.shape, 1)
            inside = lane < 8 * HALF
            rest = jnp.concatenate(tiles[HALF:], axis=0)
            rest = jnp.where(inside, 0.0, rest) - exact(
                done[:, 8 * HALF :], jnp.where(inside & (lane > row), 0.0, done), dims(0, 0)
            )
            tiles[HALF:] = [rest[8 * i : 8 * i + 8, :] for i in range(HALF)]
    for i in range(NB // 8):
        z_ref[8 * i : 8 * i + 8, :] = tiles[i]


def invert_cholesky(z_ref, d_ref, between):
    lower = lax.broadcasted_iota(jnp.int32, (NB, NB), 0) >= lax.broadcasted_iota(
        jnp.int32, (NB, NB), 1
    )
    for b in range(R // NB):
        lo, hi = b * NB, (b + 1) * NB
        d_ref[...] = z_ref[lo:hi, lo:hi]
        invert_leaf(d_ref, lambda: between(2 * b))
        block = jnp.where(lower, d_ref[...], 0.0)
        z_ref[lo:hi, lo:hi] = block
        if b:
            z_ref[lo:hi, :lo] = exact(block, z_ref[lo:hi, :lo], dims(1, 0))
        if hi < R:
            upper = exact(block, z_ref[lo:hi, hi:], dims(1, 0))
            z_ref[lo:hi, hi:] = upper
            z_ref[hi:, lo:hi] = jnp.zeros((R - hi, NB), F32)
            z_ref[hi:, :] -= exact(upper, z_ref[lo:hi, :], dims(0, 0))
            z_ref[lo:hi, hi:] = jnp.zeros((NB, R - hi), F32)
        between(2 * b + 1)


class Copies:
    def __init__(self, send_sems, recv_sems):
        self.send_sems, self.recv_sems = send_sems, recv_sems
        self.count = 0
        self.unfinished = []

    def start(self, src, dst, device):
        i = self.count
        self.count += 1
        copy = pltpu.make_async_remote_copy(
            src_ref=src,
            dst_ref=dst,
            send_sem=self.send_sems.at[i],
            recv_sem=self.recv_sems.at[i],
            device_id=device,
            device_id_type=MESH,
        )
        copy.start()
        self.unfinished.append(copy)
        return copy

    def finish(self):
        for copy in self.unfinished:
            copy.wait_send()


class Ring:
    def __init__(self, copies, place, right, left, columns=slice(None)):
        self.copies, self.place, self.right, self.left = copies, place, right, left
        self.columns = columns

    def rows(self, base, size, ahead, part=None):
        start = base + size * lax.rem(self.place + ahead, 4)
        if part is None:
            return pl.ds(pl.multiple_of(start, 8), size)
        return pl.ds(pl.multiple_of(start + part * (size // 2), 8), size // 2)

    def scatter_far(self, src, base, size, far, near):
        self.src, self.base, self.size, self.far, self.near = src, base, size, far, near
        start, cols = self.copies.start, self.columns
        self.far_right = start(
            src.at[self.rows(base, size, 2, 0), cols], far.at[0, :, cols], self.right
        )
        self.far_left = start(
            src.at[self.rows(base, size, 2, 1), cols], far.at[1, :, cols], self.left
        )

    def scatter_near(self):
        src, base, size, near, cols = self.src, self.base, self.size, self.near, self.columns
        half = size // 2
        self.near_right = self.copies.start(
            src.at[self.rows(base, size, 1, 1), cols], near.at[0, half:, cols], self.right
        )
        self.near_left = self.copies.start(
            src.at[self.rows(base, size, 3, 0), cols], near.at[1, :half, cols], self.left
        )

    def scatter_start(self, *args):
        self.scatter_far(*args)
        self.scatter_near()

    def scatter_middle(self):
        half, cols = self.size // 2, self.columns
        self.far_right.wait_recv()
        rows = self.rows(self.base, self.size, 1, 0)
        self.src[rows, cols] += self.far[0, :, cols]
        self.last_right = self.copies.start(
            self.src.at[rows, cols], self.near.at[0, :half, cols], self.right
        )
        self.far_left.wait_recv()
        rows = self.rows(self.base, self.size, 3, 1)
        self.src[rows, cols] += self.far[1, :, cols]
        self.last_left = self.copies.start(
            self.src.at[rows, cols], self.near.at[1, half:, cols], self.left
        )

    def scatter_end(self, out, out_rows):
        cols = self.columns
        for copy in (self.near_right, self.near_left, self.last_right, self.last_left):
            copy.wait_recv()
        own = self.src[self.rows(self.base, self.size, 0), cols]
        out[out_rows, cols] = own + self.near[0, :, cols] + self.near[1, :, cols]

    def gather_start(self, buf, base, size):
        self.buf, self.base, self.size = buf, base, size
        own = buf.at[self.rows(base, size, 0), self.columns]
        self.to_right = self.copies.start(own, own, self.right)
        self.to_left = self.copies.start(own, own, self.left)

    def gather_middle(self):
        self.to_right.wait_recv()
        part = self.buf.at[self.rows(self.base, self.size, 3, 0), self.columns]
        self.on_right = self.copies.start(part, part, self.right)
        self.to_left.wait_recv()
        part = self.buf.at[self.rows(self.base, self.size, 1, 1), self.columns]
        self.on_left = self.copies.start(part, part, self.left)

    def gather_end(self):
        self.on_right.wait_recv()
        self.on_left.wait_recv()


BLOCKS = [(i, j) for i in range(R // NB) for j in range(i, R // NB)]
PACKED = len(BLOCKS) * NB
LIMIT = 42 * 1024 * 1024
COPIES = 160
PIECE = PACKED // 32
CHUNKS = [slice(0, R // 2), slice(R // 2, R)]


def kernel(
    momentum, gradient, weight, basis,
    right_out, scaled_out, high_out, low_out, buffer_out, weight_out,
    mom, grad, prev, high, low, high_t, low_t,
    part, first_a, first_b, left, far_x, near_x, far_z, near_z, far_x2, near_x2, far_z2, near_z2,
    gram, packed, packed_sum, gram_in, gram_y,
    right, right_in, right_sum, right_far, right_near,
    tri, block, tri_h, tri_l, squares,
    load_sems, send_sems, recv_sems,
):
    r, c = lax.axis_index("row"), lax.axis_index("col")
    y, core = r // 2, lax.rem(r, 2)
    z, x = c // 4, lax.rem(c, 4)

    def at(dy=0, dz=0, dx=0):
        return (
            lax.rem(y + dy, 4) * 2 + core,
            lax.rem(z + dz, 4) * 4 + lax.rem(x + dx, 4),
        )

    sibling = (y * 2 + 1 - core, c)

    order = []
    for ahead in (2, 1, 3, 0):
        order.append(lax.rem(x + ahead, 4) * SLICE)
        order.append(ROWS // 2 + lax.rem(z + ahead, 4) * SLICE)
    order = [pl.ds(pl.multiple_of(start, SLICE), SLICE) for start in order]
    load_basis = pltpu.make_async_copy(basis, prev, load_sems.at[16])
    load_basis.start()
    loads = []
    for i, rows in enumerate(order):
        a = pltpu.make_async_copy(momentum.at[rows], mom.at[rows], load_sems.at[2 * i])
        b = pltpu.make_async_copy(gradient.at[rows], grad.at[rows], load_sems.at[2 * i + 1])
        a.start()
        b.start()
        loads.append((a, b))

    barrier = pltpu.get_barrier_semaphore()
    peers = [sibling, at(dy=1), at(dy=2), at(dy=3)] + [(r, lax.rem(c + k, 16)) for k in range(1, 16)]
    for peer in peers:
        pl.semaphore_signal(barrier, inc=1, device_id=peer, device_id_type=MESH)

    copies = Copies(send_sems, recv_sems)
    x_ring = lambda cols: Ring(copies, x, at(dx=1), at(dx=3), cols)
    z_ring = lambda cols: Ring(copies, z, at(dz=1), at(dz=3), cols)
    outer = [(x_ring(cols), z_ring(cols)) for cols in CHUNKS]
    inner = [(z_ring(cols), x_ring(cols)) for cols in CHUNKS]
    rings_w = [Ring(copies, y, at(dy=1), at(dy=3), cols) for cols in CHUNKS]

    def partial_left(i):
        rows = order[i]
        for load in loads[i]:
            load.wait()
        buffer = mom[rows, :] + grad[rows, :].astype(F32)
        buffer_out[rows, :] = buffer
        h, l = split(buffer)
        high[rows, :] = h
        low[rows, :] = l
        both = dot(jnp.concatenate([h, l], axis=0), prev[...])
        part[rows, :] = both[:SLICE] + both[SLICE:]

    load_basis.wait()
    for i in range(2):
        partial_left(i)
    pl.semaphore_wait(barrier, len(peers))
    for a, b in outer:
        a.scatter_far(part, 0, SLICE, far_x, near_x)
        b.scatter_far(part, ROWS // 2, SLICE, far_z, near_z)
    for i in range(2, 6):
        partial_left(i)
    for a, b in outer:
        a.scatter_near()
        b.scatter_near()
    for i in range(6, 8):
        partial_left(i)
    for a, b in outer:
        a.scatter_middle()
        b.scatter_middle()

    load_weight = pltpu.make_async_copy(weight, weight_out, load_sems.at[17])
    load_weight.start()

    @pl.loop(0, ROWS // NB)
    def _(k):
        rows = pl.ds(pl.multiple_of(k * NB, NB), NB)
        high_t[:, rows] = high[rows, :].T
        low_t[:, rows] = low[rows, :].T

    everything = pl.ds(0, SLICE)
    for (a, b), (a2, b2) in zip(outer, inner):
        a.scatter_end(first_a, everything)
        a2.scatter_start(first_a, 0, SUB, far_z2, near_z2)
        b.scatter_end(first_b, everything)
        b2.scatter_start(first_b, 0, SUB, far_x2, near_x2)
    for a2, b2 in inner:
        a2.scatter_middle()
        b2.scatter_middle()
    base_a = x * SLICE
    base_b = ROWS // 2 + z * SLICE
    for a2, b2 in inner:
        a2.scatter_end(left, a2.rows(base_a, SUB, 0))
        a2.gather_start(left, base_a, SUB)
        b2.scatter_end(left, b2.rows(base_b, SUB, 0))
        b2.gather_start(left, base_b, SUB)
    for a2, b2 in inner:
        a2.gather_middle()
        b2.gather_middle()
    for (a, b), (a2, b2) in zip(outer, inner):
        a2.gather_end()
        a.gather_start(left, 0, SLICE)
        b2.gather_end()
        b.gather_start(left, ROWS // 2, SLICE)

    def slices(ahead):
        return (
            pl.ds(pl.multiple_of(lax.rem(x + ahead, 4) * SLICE, SLICE), SLICE),
            pl.ds(pl.multiple_of(ROWS // 2 + lax.rem(z + ahead, 4) * SLICE, SLICE), SLICE),
        )

    def halves(ahead):
        a, b = slices(ahead)
        return split(jnp.concatenate([left[a, :], left[b, :]], axis=0))

    def add_gram(ahead, first):
        h, l = halves(ahead)
        for i in range(R // NB):
            lo, hi = i * NB, (i + 1) * NB
            hl, ll = h[:, lo:hi], l[:, lo:hi]
            term = dot_t(hl, h[:, lo:]) + (
                dot_t(hl, l[:, lo:]) + dot_t(ll, h[:, lo:]) + dot_t(ll, l[:, lo:])
            )
            if first:
                gram[lo:hi, lo:] = term
            else:
                gram[lo:hi, lo:] += term

    def add_right(ahead, first):
        a, b = slices(ahead)
        h, l = halves(ahead)

        @pl.loop(0, COLS // 256)
        def _(k):
            rows = pl.ds(pl.multiple_of(k * 256, 256), 256)
            bh = jnp.concatenate([high_t[rows, a], high_t[rows, b]], axis=1)
            bl = jnp.concatenate([low_t[rows, a], low_t[rows, b]], axis=1)
            both = dot(jnp.concatenate([bh, bl], axis=0), h)
            term = both[:256] + (dot(bh, l) + both[256:])
            if first:
                right[rows, :] = term
            else:
                right[rows, :] += term

    add_gram(0, True)
    add_right(0, True)
    for a, b in outer:
        a.gather_middle()
        b.gather_middle()
    add_gram(1, False)
    add_gram(3, False)
    add_right(1, False)
    add_right(3, False)
    for a, b in outer:
        a.gather_end()
        b.gather_end()
    add_gram(2, False)

    for k, (i, j) in enumerate(BLOCKS):
        packed[k * NB : (k + 1) * NB, :] = gram[i * NB : (i + 1) * NB, j * NB : (j + 1) * NB]

    def half_of(whole, which):
        return pl.ds(pl.multiple_of(which * (whole // 2), 8), whole // 2)

    mine_g = half_of(PACKED, core)
    mine_w, other_w = half_of(COLS, core), half_of(COLS, 1 - core)

    def piece(which, of):
        return pl.ds(pl.multiple_of(which * (PACKED // 2) + of * PIECE, 8), PIECE)

    swap_g = copies.start(packed.at[piece(1 - core, c)], gram_in, sibling)
    add_right(2, False)
    swaps_w = [
        copies.start(right.at[other_w, cols], right_in.at[:, cols], sibling)
        for cols in CHUNKS
    ]
    swap_g.wait_recv()
    gram_y[y] = packed[piece(core, c), :] + gram_in[...]
    over_y = [copies.start(gram_y.at[y], gram_y.at[y], at(dy=k)) for k in (2, 1, 3)]
    for cols, swap, ring in zip(CHUNKS, swaps_w, rings_w):
        swap.wait_recv()
        right[mine_w, cols] += right_in[:, cols]
        ring.scatter_far(right, core * (COLS // 2), COLS // 8, right_far, right_near)
    for copy in over_y:
        copy.wait_recv()
    own_piece = packed_sum.at[piece(core, c)]
    own_piece[...] = (gram_y[0] + gram_y[1]) + (gram_y[2] + gram_y[3])
    over_col = [
        copies.start(own_piece, own_piece, (r, lax.rem(c + k, 16))) for k in range(1, 16)
    ]
    for ring in rings_w:
        ring.scatter_near()
    for ring in rings_w:
        ring.scatter_middle()
    for copy in over_col:
        copy.wait_recv()
    back_g = copies.start(packed_sum.at[mine_g], packed_sum.at[mine_g], sibling)
    back_g.wait_recv()
    for k, (i, j) in enumerate(BLOCKS):
        tri[i * NB : (i + 1) * NB, j * NB : (j + 1) * NB] = packed_sum[k * NB : (k + 1) * NB, :]

    swaps = []

    def between(step):
        if step == 0:
            for ring in rings_w:
                ring.scatter_end(right_sum, ring.rows(core * (COLS // 2), COLS // 8, 0))
                ring.gather_start(right_sum, core * (COLS // 2), COLS // 8)
        elif step in (2, 4):
            rings_w[step // 2 - 1].gather_middle()
        elif step in (5, 6):
            ring = rings_w[step - 5]
            ring.gather_end()
            own = right_sum.at[mine_w, ring.columns]
            swaps.append(copies.start(own, own, sibling))

    invert_cholesky(tri, block, between)
    for swap in swaps:
        swap.wait_recv()

    tri_h[...], tri_l[...] = split(tri[...].T)
    squares[c] = jnp.zeros((8, R), F32)
    h2 = R // 2

    def solved(value):
        h, l = split(value)
        n = len(value)
        both = jnp.concatenate([h, l], axis=0)
        halves = []
        for width, out in ((h2, slice(0, h2)), (R, slice(h2, R))):
            p = dot(both[:, :width], tri_h[:width, out])
            q = dot(h[:, :width], tri_l[:width, out])
            halves.append(p[:n] + (p[n:] + q))
        return jnp.concatenate(halves, axis=1)

    @pl.loop(0, COLS // 256)
    def _(k):
        rows = pl.ds(pl.multiple_of(k * 256, 256), 256)
        value = solved(right_sum[rows, :])
        mom[rows, R:] = value
        squares[c] += jnp.sum((value * value).reshape(32, 8, R), axis=0)

    sums = []
    for k in range(1, 16):
        sums.append(copies.start(squares.at[c], squares.at[c], (r, lax.rem(c + k, 16))))

    @pl.loop(0, ROWS // 256)
    def _(k):
        rows = pl.ds(pl.multiple_of(k * 256, 256), 256)
        value = solved(left[rows, :])
        mom[rows, :R] = value
        h, l = split(value)
        high_out[rows, :] = h
        low_out[rows, :] = l

    for copy in sums:
        copy.wait_recv()
    total = squares[0]
    for k in range(1, 16):
        total = total + squares[k]
    total = jnp.sum(total, axis=0, keepdims=True)
    scale = jnp.sqrt(total / N + epsilon)
    inverse = 1.0 / scale
    right_out[...] = (mom[:, R:] * inverse).astype(BF16)
    scaled_out[...] = (mom[:, :R] * scale).astype(BF16)
    load_weight.wait()
    copies.finish()


def factors(momentum, gradient, weight, basis):
    vmem = pl.BlockSpec(memory_space=pltpu.VMEM)
    any_ = pl.BlockSpec(memory_space=pltpu.HBM)
    f = lambda *s: pltpu.VMEM(s, F32)
    b = lambda *s: pltpu.VMEM(s, BF16)
    ring = lambda s, w: [f(2, s // 2, w), f(2, s, w)]
    return pl.pallas_call(
        kernel,
        out_shape=[
            jax.ShapeDtypeStruct((COLS, R), BF16),
            jax.ShapeDtypeStruct((ROWS, R), BF16),
            jax.ShapeDtypeStruct((ROWS, R), BF16),
            jax.ShapeDtypeStruct((ROWS, R), BF16),
            jax.ShapeDtypeStruct((ROWS, COLS), F32),
            jax.ShapeDtypeStruct((ROWS, COLS), BF16),
        ],
        in_specs=[any_] * 4,
        out_specs=[vmem] * 6,
        scratch_shapes=[
            f(ROWS, COLS), b(ROWS, COLS), b(COLS, R),
            b(ROWS, COLS), b(ROWS, COLS), b(COLS, ROWS), b(COLS, ROWS),
            f(ROWS, R), f(SLICE, R), f(SLICE, R), f(ROWS, R),
            *ring(SLICE, R), *ring(SLICE, R), *ring(SUB, R), *ring(SUB, R),
            f(R, R), f(PACKED, NB), f(PACKED, NB), f(PIECE, NB), f(4, PIECE, NB),
            f(COLS, R), f(COLS // 2, R), f(COLS, R), *ring(COLS // 8, R),
            f(R, R), f(NB, NB), b(R, R), b(R, R), f(16, 8, R),
            pltpu.SemaphoreType.DMA((18,)),
            pltpu.SemaphoreType.DMA((COPIES,)),
            pltpu.SemaphoreType.DMA((COPIES,)),
        ],
        compiler_params=pltpu.CompilerParams(
            collective_id=0, has_side_effects=True, vmem_limit_bytes=LIMIT
        ),
        name="factors",
    )(momentum, gradient, weight, basis)


def last_kernel(b, w, scaled, high, low, v, basis, new_w, new_m, new_v):
    buffer = b[...]
    vs = v[...]
    rows = len(buffer)
    both = dot_nt(jnp.concatenate([scaled[...], high[...], low[...]], axis=0), vs)
    new_m[...] = buffer - decay_loss * both[:rows]
    update = both[rows : 2 * rows] + both[2 * rows :]
    rate = step_size * (M / N) ** 0.5
    new_w[...] = (w[...].astype(F32) - rate * update).astype(BF16)
    new_v[...] = basis[...]


def outputs(buffer, weight, scaled, high, low, v):
    rows = 256
    wide = pl.BlockSpec((rows, COLS), lambda i: (i, 0))
    thin = pl.BlockSpec((rows, R), lambda i: (i, 0))
    whole = pl.BlockSpec((COLS, R), lambda i: (0, 0))
    return pl.pallas_call(
        last_kernel,
        grid=(ROWS // rows,),
        out_shape=[
            jax.ShapeDtypeStruct((ROWS, COLS), BF16),
            jax.ShapeDtypeStruct((ROWS, COLS), F32),
            jax.ShapeDtypeStruct((COLS, R), BF16),
        ],
        in_specs=[wide, wide, thin, thin, thin, whole, thin],
        out_specs=[wide, wide, thin],
        compiler_params=pltpu.CompilerParams(vmem_limit_bytes=20 * 1024 * 1024),
        name="outputs",
    )(buffer, weight, scaled, high, low, v, v)


def per_device(weight, momentum, gradient, prev_basis):
    kept = [
        pltpu.with_memory_space_constraint(a, pltpu.HBM)
        for a in (momentum, gradient, weight, prev_basis)
    ]
    v, *rest, buffer, held = factors(*kept)
    return tuple(outputs(buffer, held, *rest, v))


def solution(mesh):
    return jax.shard_map(
        per_device,
        mesh=mesh,
        in_specs=(P("row", "col"), P("row", "col"), P("row", "col"), P("col", None)),
        out_specs=(P("row", "col"), P("row", "col"), P("col", None)),
        check_vma=False,
    )
```

```python
import functools

import jax
import jax.numpy as jnp
from jax import lax
from jax.experimental import pallas as pl
from jax.experimental.pallas import tpu as pltpu
from jax.sharding import PartitionSpec as P

MESH = pl.DeviceIdType.MESH
F32 = jnp.float32
BF16 = jnp.bfloat16

M = 8192
N = 16384
R = 512
ROWS = 1024
COLS = 1024
NB = 128
SLICE = 128
SUB = 32

decay_loss = 0.1
step_size = 0.4
epsilon = 1e-06


def dims(a, b):
    return (((a,), (b,)), ((), ()))


def dot(a, b):
    return jnp.dot(a, b, preferred_element_type=F32)


def dot_t(a, b):
    return lax.dot_general(a, b, dims(0, 0), preferred_element_type=F32)


def dot_nt(a, b):
    return lax.dot_general(a, b, dims(1, 1), preferred_element_type=F32)


def split(x):
    high = x.astype(BF16)
    return high, (x - high.astype(F32)).astype(BF16)


def from_row(x, i):
    return jnp.broadcast_to(x[i : i + 1, :], x.shape)


def from_lane(x, k):
    return jnp.broadcast_to(x[:, k : k + 1], (8, NB))


GROUP = 8
NEAR = 7


def exact(a, b, contract):
    return lax.dot_general(
        a, b, contract, precision=lax.Precision.HIGHEST, preferred_element_type=F32
    )


def invert_leaf(z_ref, between, rest):
    rows = lax.broadcasted_iota(jnp.int32, (8, NB), 0)
    lanes = lax.broadcasted_iota(jnp.int32, (8, NB), 1)
    tiles = [z_ref[8 * i : 8 * i + 8, :] for i in range(NB // 8)]
    for p in range(NB // 8):
        if rest:
            rest.pop(0)()
        tile = tiles[p]
        columns = [from_lane(tile, 8 * p + k) for k in range(8)]
        own = (lanes >= 8 * p) & (lanes < 8 * p + 8)
        tile = jnp.where(own, jnp.where(lanes - 8 * p == rows, 1.0, 0.0), tile)
        below = tiles[p + 1 : (p // GROUP + 1) * GROUP]
        near = [[from_lane(t, 8 * p + k) for k in range(8)] for t in below[:NEAR]]
        upper, factors = [], [[] for _ in near]
        for j in range(8):
            inverse = lax.rsqrt(from_row(columns[j], j))
            t = columns[j] * inverse
            masked = jnp.where(rows > j, t, 0.0)
            u = from_row(tile, j) * inverse
            upper.append(u)
            tile = jnp.where(rows == j, u, tile - masked * u)
            for n, f in zip(near, factors):
                f.append(n[j] * inverse)
            for k in range(j + 1, 8):
                tk = from_row(t, k)
                columns[k] = columns[k] - masked * tk
                for n, f in zip(near, factors):
                    n[k] = n[k] - f[j] * tk
        tiles[p] = tile

        def eliminated(x, factors):
            terms = [t * u for t, u in zip(factors, upper)]
            while len(terms) > 1:
                terms = [terms[i] + terms[i + 1] for i in range(0, len(terms), 2)]
            return jnp.where(own, 0.0, x) - terms[0]

        for i, (t, f) in enumerate(zip(below, factors)):
            tiles[p + 1 + i] = eliminated(t, f)
        if len(below) > NEAR:
            turned = tile.T
            for i in range(p + 1 + NEAR, p + 1 + len(below)):
                part = turned[8 * i : 8 * i + 8, :]
                tiles[i] = eliminated(tiles[i], [from_lane(part, k) for k in range(8)])
        if p + 1 == NB // 16:
            between()
        if (p + 1) % GROUP == 0 and p + 1 < NB // 8:
            top, end = p + 1 - GROUP, p + 1
            done = jnp.concatenate(tiles[top:end], axis=0)
            row = 8 * top + lax.broadcasted_iota(jnp.int32, done.shape, 0)
            lane = lax.broadcasted_iota(jnp.int32, done.shape, 1)
            inside = (lane >= 8 * top) & (lane < 8 * end)
            later = jnp.concatenate(tiles[end:], axis=0)
            lane2 = lax.broadcasted_iota(jnp.int32, later.shape, 1)
            later = jnp.where((lane2 >= 8 * top) & (lane2 < 8 * end), 0.0, later) - exact(
                done[:, 8 * end :], jnp.where(inside & (lane > row), 0.0, done), dims(0, 0)
            )
            tiles[end:] = [later[8 * i : 8 * i + 8, :] for i in range(NB // 8 - end)]
    for i in range(NB // 8):
        z_ref[8 * i : 8 * i + 8, :] = tiles[i]


def invert_cholesky(z_ref, d_ref, between):
    lower = lax.broadcasted_iota(jnp.int32, (NB, NB), 0) >= lax.broadcasted_iota(
        jnp.int32, (NB, NB), 1
    )
    rest = []
    for b in range(R // NB):
        lo, hi = b * NB, (b + 1) * NB
        d_ref[...] = z_ref[lo:hi, lo:hi]
        invert_leaf(d_ref, lambda: between(2 * b), rest)
        while rest:
            rest.pop(0)()
        block = jnp.where(lower, d_ref[...], 0.0)
        z_ref[lo:hi, lo:hi] = block
        if hi < R:
            follow = slice(hi, hi + NB)
            first = exact(block, z_ref[lo:hi, follow], dims(1, 0))
            z_ref[follow, follow] -= exact(first, first, dims(0, 0))
            z_ref[lo:hi, follow] = first
        rest = later_work(z_ref, lo, hi, block)
        between(2 * b + 1)
    while rest:
        rest.pop(0)()
    for b in range(R // NB - 1):
        z_ref[b * NB : (b + 1) * NB, (b + 1) * NB :] = jnp.zeros((NB, R - (b + 1) * NB), F32)


def later_work(z_ref, lo, hi, block):
    parts = []
    if lo:

        def own_rows():
            z_ref[lo:hi, :lo] = exact(block, z_ref[lo:hi, :lo], dims(1, 0))

        parts.append(own_rows)
    if hi + NB < R:

        def upper_rows():
            z_ref[lo:hi, hi + NB :] = exact(block, z_ref[lo:hi, hi + NB :], dims(1, 0))

        parts.append(upper_rows)
    for i in range(hi, R, NB):
        rows = slice(i, i + NB)

        def inverse_part(rows=rows):
            zero = jnp.zeros((NB, NB), F32)
            before = jnp.concatenate([z_ref[rows, :lo], zero], axis=1) if lo else zero
            z_ref[rows, :hi] = before - exact(
                z_ref[lo:hi, rows], z_ref[lo:hi, :hi], dims(0, 0)
            )

        def upper_part(rows=rows, start=i + NB if i == hi else i):
            z_ref[rows, start:] -= exact(z_ref[lo:hi, rows], z_ref[lo:hi, start:], dims(0, 0))

        parts.append(inverse_part)
        if i + NB < R or i > hi:
            parts.append(upper_part)
    return parts


class Copies:
    def __init__(self, send_sems, recv_sems):
        self.send_sems, self.recv_sems = send_sems, recv_sems
        self.count = 0
        self.unfinished = []

    def start(self, src, dst, device):
        i = self.count
        self.count += 1
        copy = pltpu.make_async_remote_copy(
            src_ref=src,
            dst_ref=dst,
            send_sem=self.send_sems.at[i],
            recv_sem=self.recv_sems.at[i],
            device_id=device,
            device_id_type=MESH,
        )
        copy.start()
        self.unfinished.append(copy)
        return copy

    def finish(self):
        for copy in self.unfinished:
            copy.wait_send()


class Ring:
    def __init__(self, copies, place, right, left, columns=slice(None)):
        self.copies, self.place, self.right, self.left = copies, place, right, left
        self.columns = columns

    def rows(self, base, size, ahead, part=None):
        start = base + size * lax.rem(self.place + ahead, 4)
        if part is None:
            return pl.ds(pl.multiple_of(start, 8), size)
        return pl.ds(pl.multiple_of(start + part * (size // 2), 8), size // 2)

    def scatter_far(self, src, base, size, far, near):
        self.src, self.base, self.size, self.far, self.near = src, base, size, far, near
        start, cols = self.copies.start, self.columns
        self.far_right = start(
            src.at[self.rows(base, size, 2, 0), cols], far.at[0, :, cols], self.right
        )
        self.far_left = start(
            src.at[self.rows(base, size, 2, 1), cols], far.at[1, :, cols], self.left
        )

    def scatter_near(self):
        src, base, size, near, cols = self.src, self.base, self.size, self.near, self.columns
        half = size // 2
        self.near_right = self.copies.start(
            src.at[self.rows(base, size, 1, 1), cols], near.at[0, half:, cols], self.right
        )
        self.near_left = self.copies.start(
            src.at[self.rows(base, size, 3, 0), cols], near.at[1, :half, cols], self.left
        )

    def scatter_start(self, *args):
        self.scatter_far(*args)
        self.scatter_near()

    def scatter_middle(self):
        half, cols = self.size // 2, self.columns
        self.far_right.wait_recv()
        rows = self.rows(self.base, self.size, 1, 0)
        self.src[rows, cols] += self.far[0, :, cols]
        self.last_right = self.copies.start(
            self.src.at[rows, cols], self.near.at[0, :half, cols], self.right
        )
        self.far_left.wait_recv()
        rows = self.rows(self.base, self.size, 3, 1)
        self.src[rows, cols] += self.far[1, :, cols]
        self.last_left = self.copies.start(
            self.src.at[rows, cols], self.near.at[1, half:, cols], self.left
        )

    def scatter_end(self, out, out_rows):
        cols = self.columns
        for copy in (self.near_right, self.near_left, self.last_right, self.last_left):
            copy.wait_recv()
        own = self.src[self.rows(self.base, self.size, 0), cols]
        out[out_rows, cols] = own + self.near[0, :, cols] + self.near[1, :, cols]

    def gather_start(self, buf, base, size):
        self.buf, self.base, self.size = buf, base, size
        own = buf.at[self.rows(base, size, 0), self.columns]
        self.to_right = self.copies.start(own, own, self.right)
        self.to_left = self.copies.start(own, own, self.left)

    def gather_middle(self):
        self.to_right.wait_recv()
        part = self.buf.at[self.rows(self.base, self.size, 3, 0), self.columns]
        self.on_right = self.copies.start(part, part, self.right)
        self.to_left.wait_recv()
        part = self.buf.at[self.rows(self.base, self.size, 1, 1), self.columns]
        self.on_left = self.copies.start(part, part, self.left)

    def gather_end(self):
        self.on_right.wait_recv()
        self.on_left.wait_recv()


BLOCKS = [(i, j) for i in range(R // NB) for j in range(i, R // NB)]
PACKED = len(BLOCKS) * NB
LIMIT = 42 * 1024 * 1024
COPIES = 160
PIECE = PACKED // 32
CHUNKS = [slice(0, R // 2), slice(R // 2, R)]


def kernel(
    momentum, gradient, weight, basis,
    right_out, scaled_out, high_out, low_out, buffer_out, weight_out,
    mom, grad, prev, high, low, high_t, low_t,
    part, first_a, first_b, left, far_x, near_x, far_z, near_z, far_x2, near_x2, far_z2, near_z2,
    gram, packed, packed_sum, gram_in, gram_y,
    right, right_in, right_sum, right_far, right_near,
    tri, block, tri_h, tri_l, squares, square_rows,
    load_sems, send_sems, recv_sems,
):
    r, c = lax.axis_index("row"), lax.axis_index("col")
    y, core = r // 2, lax.rem(r, 2)
    z, x = c // 4, lax.rem(c, 4)

    def at(dy=0, dz=0, dx=0):
        return (
            lax.rem(y + dy, 4) * 2 + core,
            lax.rem(z + dz, 4) * 4 + lax.rem(x + dx, 4),
        )

    sibling = (y * 2 + 1 - core, c)

    order = []
    for ahead in (2, 1, 3, 0):
        order.append(lax.rem(x + ahead, 4) * SLICE)
        order.append(ROWS // 2 + lax.rem(z + ahead, 4) * SLICE)
    order = [pl.ds(pl.multiple_of(start, SLICE), SLICE) for start in order]
    load_basis = pltpu.make_async_copy(basis, prev, load_sems.at[16])
    load_basis.start()
    loads = []
    for i, rows in enumerate(order):
        a = pltpu.make_async_copy(momentum.at[rows], mom.at[rows], load_sems.at[2 * i])
        b = pltpu.make_async_copy(gradient.at[rows], grad.at[rows], load_sems.at[2 * i + 1])
        a.start()
        b.start()
        loads.append((a, b))

    barrier = pltpu.get_barrier_semaphore()
    peers = [sibling, at(dy=1), at(dy=2), at(dy=3)] + [(r, lax.rem(c + k, 16)) for k in range(1, 16)]
    for peer in peers:
        pl.semaphore_signal(barrier, inc=1, device_id=peer, device_id_type=MESH)

    copies = Copies(send_sems, recv_sems)
    x_ring = lambda cols: Ring(copies, x, at(dx=1), at(dx=3), cols)
    z_ring = lambda cols: Ring(copies, z, at(dz=1), at(dz=3), cols)
    outer = [(x_ring(cols), z_ring(cols)) for cols in CHUNKS]
    inner = [(z_ring(cols), x_ring(cols)) for cols in CHUNKS]
    rings_w = [Ring(copies, y, at(dy=1), at(dy=3), cols) for cols in CHUNKS]

    def partial_left(i):
        rows = order[i]
        for load in loads[i]:
            load.wait()
        buffer = mom[rows, :] + grad[rows, :].astype(F32)
        buffer_out[rows, :] = buffer
        h, l = split(buffer)
        high[rows, :] = h
        low[rows, :] = l
        both = dot(jnp.concatenate([h, l], axis=0), prev[...])
        part[rows, :] = both[:SLICE] + both[SLICE:]

    load_basis.wait()
    for i in range(2):
        partial_left(i)
    pl.semaphore_wait(barrier, len(peers))
    for a, b in outer:
        a.scatter_far(part, 0, SLICE, far_x, near_x)
        b.scatter_far(part, ROWS // 2, SLICE, far_z, near_z)
    for i in range(2, 6):
        partial_left(i)
    for a, b in outer:
        a.scatter_near()
        b.scatter_near()
    for i in range(6, 8):
        partial_left(i)
    for a, b in outer:
        a.scatter_middle()
        b.scatter_middle()

    load_weight = pltpu.make_async_copy(weight, weight_out, load_sems.at[17])
    load_weight.start()

    @pl.loop(0, ROWS // NB)
    def _(k):
        rows = pl.ds(pl.multiple_of(k * NB, NB), NB)
        high_t[:, rows] = high[rows, :].T
        low_t[:, rows] = low[rows, :].T

    everything = pl.ds(0, SLICE)
    for (a, b), (a2, b2) in zip(outer, inner):
        a.scatter_end(first_a, everything)
        a2.scatter_start(first_a, 0, SUB, far_z2, near_z2)
        b.scatter_end(first_b, everything)
        b2.scatter_start(first_b, 0, SUB, far_x2, near_x2)
    for a2, b2 in inner:
        a2.scatter_middle()
        b2.scatter_middle()
    base_a = x * SLICE
    base_b = ROWS // 2 + z * SLICE
    for a2, b2 in inner:
        a2.scatter_end(left, a2.rows(base_a, SUB, 0))
        a2.gather_start(left, base_a, SUB)
        b2.scatter_end(left, b2.rows(base_b, SUB, 0))
        b2.gather_start(left, base_b, SUB)
    for a2, b2 in inner:
        a2.gather_middle()
        b2.gather_middle()
    for (a, b), (a2, b2) in zip(outer, inner):
        a2.gather_end()
        a.gather_start(left, 0, SLICE)
        b2.gather_end()
        b.gather_start(left, ROWS // 2, SLICE)

    def slices(ahead):
        return (
            pl.ds(pl.multiple_of(lax.rem(x + ahead, 4) * SLICE, SLICE), SLICE),
            pl.ds(pl.multiple_of(ROWS // 2 + lax.rem(z + ahead, 4) * SLICE, SLICE), SLICE),
        )

    def halves(ahead):
        a, b = slices(ahead)
        return split(jnp.concatenate([left[a, :], left[b, :]], axis=0))

    def add_gram(ahead, first):
        h, l = halves(ahead)
        for i in range(R // NB):
            lo, hi = i * NB, (i + 1) * NB
            hl, ll = h[:, lo:hi], l[:, lo:hi]
            term = dot_t(hl, h[:, lo:]) + (
                dot_t(hl, l[:, lo:]) + dot_t(ll, h[:, lo:]) + dot_t(ll, l[:, lo:])
            )
            if first:
                gram[lo:hi, lo:] = term
            else:
                gram[lo:hi, lo:] += term

    def add_right(ahead, first, start=0, count=COLS):
        a, b = slices(ahead)
        h, l = halves(ahead)

        @pl.loop(0, count // 256)
        def _(k):
            rows = pl.ds(pl.multiple_of(start + k * 256, 256), 256)
            bh = jnp.concatenate([high_t[rows, a], high_t[rows, b]], axis=1)
            bl = jnp.concatenate([low_t[rows, a], low_t[rows, b]], axis=1)
            both = dot(jnp.concatenate([bh, bl], axis=0), h)
            term = both[:256] + (dot(bh, l) + both[256:])
            if first:
                right[rows, :] = term
            else:
                right[rows, :] += term

    add_gram(0, True)
    add_right(0, True)
    for a, b in outer:
        a.gather_middle()
        b.gather_middle()
    add_gram(1, False)
    add_gram(3, False)
    add_right(1, False)
    add_right(3, False)
    for a, b in outer:
        a.gather_end()
        b.gather_end()
    add_gram(2, False)

    for k, (i, j) in enumerate(BLOCKS):
        packed[k * NB : (k + 1) * NB, :] = gram[i * NB : (i + 1) * NB, j * NB : (j + 1) * NB]

    def half_of(whole, which):
        return pl.ds(pl.multiple_of(which * (whole // 2), 8), whole // 2)

    mine_g = half_of(PACKED, core)
    mine_w, other_w = half_of(COLS, core), half_of(COLS, 1 - core)

    def piece(which, of):
        return pl.ds(pl.multiple_of(which * (PACKED // 2) + of * PIECE, 8), PIECE)

    swap_g = copies.start(packed.at[piece(1 - core, c)], gram_in, sibling)
    add_right(2, False, (1 - core) * (COLS // 2), COLS // 2)
    swaps_w = [
        copies.start(right.at[other_w, cols], right_in.at[:, cols], sibling)
        for cols in CHUNKS
    ]
    add_right(2, False, core * (COLS // 2), COLS // 2)
    swap_g.wait_recv()
    gram_y[y] = packed[piece(core, c), :] + gram_in[...]
    over_y = [copies.start(gram_y.at[y], gram_y.at[y], at(dy=k)) for k in (2, 1, 3)]
    for cols, swap, ring in zip(CHUNKS, swaps_w, rings_w):
        swap.wait_recv()
        right[mine_w, cols] += right_in[:, cols]
        ring.scatter_far(right, core * (COLS // 2), COLS // 8, right_far, right_near)
    for copy in over_y:
        copy.wait_recv()
    own_piece = packed_sum.at[piece(core, c)]
    own_piece[...] = (gram_y[0] + gram_y[1]) + (gram_y[2] + gram_y[3])
    over_col = [
        copies.start(own_piece, own_piece, (r, lax.rem(c + k, 16))) for k in range(1, 16)
    ]
    for ring in rings_w:
        ring.scatter_near()
    for ring in rings_w:
        ring.scatter_middle()
    for copy in over_col:
        copy.wait_recv()
    back_g = copies.start(packed_sum.at[mine_g], packed_sum.at[mine_g], sibling)
    back_g.wait_recv()
    for k, (i, j) in enumerate(BLOCKS):
        tri[i * NB : (i + 1) * NB, j * NB : (j + 1) * NB] = packed_sum[k * NB : (k + 1) * NB, :]

    swaps = []

    def between(step):
        if step == 0:
            for ring in rings_w:
                ring.scatter_end(right_sum, ring.rows(core * (COLS // 2), COLS // 8, 0))
                ring.gather_start(right_sum, core * (COLS // 2), COLS // 8)
        elif step in (2, 4):
            rings_w[step // 2 - 1].gather_middle()
        elif step in (5, 6):
            ring = rings_w[step - 5]
            ring.gather_end()
            own = right_sum.at[mine_w, ring.columns]
            swaps.append(copies.start(own, own, sibling))

    invert_cholesky(tri, block, between)
    for swap in swaps:
        swap.wait_recv()

    tri_h[...], tri_l[...] = split(tri[...].T)
    square_rows[...] = jnp.zeros((8, R), F32)
    h2 = R // 2

    def solved(value):
        h, l = split(value)
        n = len(value)
        both = jnp.concatenate([h, l], axis=0)
        halves = []
        for width, out in ((h2, slice(0, h2)), (R, slice(h2, R))):
            p = dot(both[:, :width], tri_h[:width, out])
            q = dot(h[:, :width], tri_l[:width, out])
            halves.append(p[:n] + (p[n:] + q))
        return jnp.concatenate(halves, axis=1)

    @pl.loop(0, COLS // 256)
    def _(k):
        rows = pl.ds(pl.multiple_of(k * 256, 256), 256)
        value = solved(right_sum[rows, :])
        mom[rows, R:] = value
        square_rows[...] += jnp.sum((value * value).reshape(32, 8, R), axis=0)

    row = jnp.sum(square_rows[...], axis=0, keepdims=True)
    quarters = [row[:, i : i + NB] for i in range(0, R, NB)]
    squares[c] = jnp.concatenate(quarters + [jnp.zeros((4, NB), F32)], axis=0)
    sums = []
    for k in range(1, 16):
        sums.append(copies.start(squares.at[c], squares.at[c], (r, lax.rem(c + k, 16))))

    @pl.loop(0, ROWS // 256)
    def _(k):
        rows = pl.ds(pl.multiple_of(k * 256, 256), 256)
        value = solved(left[rows, :])
        mom[rows, :R] = value
        h, l = split(value)
        high_out[rows, :] = h
        low_out[rows, :] = l

    for copy in sums:
        copy.wait_recv()
    total = squares[0]
    for k in range(1, 16):
        total = total + squares[k]
    total = jnp.concatenate([total[i : i + 1, :] for i in range(R // NB)], axis=1)
    scale = jnp.sqrt(total / N + epsilon)
    inverse = 1.0 / scale
    right_out[...] = (mom[:, R:] * inverse).astype(BF16)
    scaled_out[...] = (mom[:, :R] * scale).astype(BF16)
    load_weight.wait()
    copies.finish()


def factors(momentum, gradient, weight, basis):
    vmem = pl.BlockSpec(memory_space=pltpu.VMEM)
    any_ = pl.BlockSpec(memory_space=pltpu.HBM)
    f = lambda *s: pltpu.VMEM(s, F32)
    b = lambda *s: pltpu.VMEM(s, BF16)
    ring = lambda s, w: [f(2, s // 2, w), f(2, s, w)]
    return pl.pallas_call(
        kernel,
        out_shape=[
            jax.ShapeDtypeStruct((COLS, R), BF16),
            jax.ShapeDtypeStruct((ROWS, R), BF16),
            jax.ShapeDtypeStruct((ROWS, R), BF16),
            jax.ShapeDtypeStruct((ROWS, R), BF16),
            jax.ShapeDtypeStruct((ROWS, COLS), F32),
            jax.ShapeDtypeStruct((ROWS, COLS), BF16),
        ],
        in_specs=[any_] * 4,
        out_specs=[vmem] * 6,
        scratch_shapes=[
            f(ROWS, COLS), b(ROWS, COLS), b(COLS, R),
            b(ROWS, COLS), b(ROWS, COLS), b(COLS, ROWS), b(COLS, ROWS),
            f(ROWS, R), f(SLICE, R), f(SLICE, R), f(ROWS, R),
            *ring(SLICE, R), *ring(SLICE, R), *ring(SUB, R), *ring(SUB, R),
            f(R, R), f(PACKED, NB), f(PACKED, NB), f(PIECE, NB), f(4, PIECE, NB),
            f(COLS, R), f(COLS // 2, R), f(COLS, R), *ring(COLS // 8, R),
            f(R, R), f(NB, NB), b(R, R), b(R, R), f(16, 8, NB), f(8, R),
            pltpu.SemaphoreType.DMA((18,)),
            pltpu.SemaphoreType.DMA((COPIES,)),
            pltpu.SemaphoreType.DMA((COPIES,)),
        ],
        compiler_params=pltpu.CompilerParams(
            collective_id=0, has_side_effects=True, vmem_limit_bytes=LIMIT
        ),
        name="factors",
    )(momentum, gradient, weight, basis)


def last_kernel(b, w, scaled, high, low, v, basis, new_w, new_m, new_v):
    buffer = b[...]
    vs = v[...]
    rows = len(buffer)
    both = dot_nt(jnp.concatenate([scaled[...], high[...], low[...]], axis=0), vs)
    new_m[...] = buffer - decay_loss * both[:rows]
    update = both[rows : 2 * rows] + both[2 * rows :]
    rate = step_size * (M / N) ** 0.5
    new_w[...] = (w[...].astype(F32) - rate * update).astype(BF16)
    new_v[...] = basis[...]


def outputs(buffer, weight, scaled, high, low, v):
    rows = 256
    wide = pl.BlockSpec((rows, COLS), lambda i: (i, 0))
    thin = pl.BlockSpec((rows, R), lambda i: (i, 0))
    whole = pl.BlockSpec((COLS, R), lambda i: (0, 0))
    return pl.pallas_call(
        last_kernel,
        grid=(ROWS // rows,),
        out_shape=[
            jax.ShapeDtypeStruct((ROWS, COLS), BF16),
            jax.ShapeDtypeStruct((ROWS, COLS), F32),
            jax.ShapeDtypeStruct((COLS, R), BF16),
        ],
        in_specs=[wide, wide, thin, thin, thin, whole, thin],
        out_specs=[wide, wide, thin],
        compiler_params=pltpu.CompilerParams(vmem_limit_bytes=20 * 1024 * 1024),
        name="outputs",
    )(buffer, weight, scaled, high, low, v, v)


def per_device(weight, momentum, gradient, prev_basis):
    kept = [
        pltpu.with_memory_space_constraint(a, pltpu.HBM)
        for a in (momentum, gradient, weight, prev_basis)
    ]
    v, *rest, buffer, held = factors(*kept)
    return tuple(outputs(buffer, held, *rest, v))


def solution(mesh):
    return jax.shard_map(
        per_device,
        mesh=mesh,
        in_specs=(P("row", "col"), P("row", "col"), P("row", "col"), P("col", None)),
        out_specs=(P("row", "col"), P("row", "col"), P("col", None)),
        check_vma=False,
    )
```

```python
import functools

import jax
import jax.numpy as jnp
from jax import lax
from jax.experimental import pallas as pl
from jax.experimental.pallas import tpu as pltpu
from jax.sharding import PartitionSpec as P

MESH = pl.DeviceIdType.MESH
F32 = jnp.float32
BF16 = jnp.bfloat16

M = 8192
N = 16384
R = 512
ROWS = 1024
COLS = 1024
NB = 128
SLICE = 128
SUB = 32

decay_loss = 0.1
step_size = 0.4
epsilon = 1e-06


def dims(a, b):
    return (((a,), (b,)), ((), ()))


def dot(a, b):
    return jnp.dot(a, b, preferred_element_type=F32)


def dot_t(a, b):
    return lax.dot_general(a, b, dims(0, 0), preferred_element_type=F32)


def dot_nt(a, b):
    return lax.dot_general(a, b, dims(1, 1), preferred_element_type=F32)


def split(x):
    high = x.astype(BF16)
    return high, (x - high.astype(F32)).astype(BF16)


def from_row(x, i):
    return jnp.broadcast_to(x[i : i + 1, :], x.shape)


def from_lane(x, k):
    return jnp.broadcast_to(x[:, k : k + 1], (8, NB))


GROUP = 8
NEAR = 7


def exact(a, b, contract):
    return lax.dot_general(
        a, b, contract, precision=lax.Precision.HIGHEST, preferred_element_type=F32
    )


def invert_leaf(z_ref, between, rest):
    rows = lax.broadcasted_iota(jnp.int32, (8, NB), 0)
    lanes = lax.broadcasted_iota(jnp.int32, (8, NB), 1)
    tiles = [z_ref[8 * i : 8 * i + 8, :] for i in range(NB // 8)]
    for p in range(NB // 8):
        if rest:
            rest.pop(0)()
        tile = tiles[p]
        columns = [from_lane(tile, 8 * p + k) for k in range(8)]
        own = (lanes >= 8 * p) & (lanes < 8 * p + 8)
        tile = jnp.where(own, jnp.where(lanes - 8 * p == rows, 1.0, 0.0), tile)
        below = tiles[p + 1 : (p // GROUP + 1) * GROUP]
        near = [[from_lane(t, 8 * p + k) for k in range(8)] for t in below[:NEAR]]
        upper, factors = [], [[] for _ in near]
        for j in range(8):
            inverse = lax.rsqrt(from_row(columns[j], j))
            t = columns[j] * inverse
            masked = jnp.where(rows > j, t, 0.0)
            u = from_row(tile, j) * inverse
            upper.append(u)
            tile = jnp.where(rows == j, u, tile - masked * u)
            for n, f in zip(near, factors):
                f.append(n[j] * inverse)
            for k in range(j + 1, 8):
                tk = from_row(t, k)
                columns[k] = columns[k] - masked * tk
                for n, f in zip(near, factors):
                    n[k] = n[k] - f[j] * tk
        tiles[p] = tile

        def eliminated(x, factors):
            terms = [t * u for t, u in zip(factors, upper)]
            while len(terms) > 1:
                terms = [terms[i] + terms[i + 1] for i in range(0, len(terms), 2)]
            return jnp.where(own, 0.0, x) - terms[0]

        for i, (t, f) in enumerate(zip(below, factors)):
            tiles[p + 1 + i] = eliminated(t, f)
        if len(below) > NEAR:
            turned = tile.T
            for i in range(p + 1 + NEAR, p + 1 + len(below)):
                part = turned[8 * i : 8 * i + 8, :]
                tiles[i] = eliminated(tiles[i], [from_lane(part, k) for k in range(8)])
        if p + 1 == NB // 16:
            between()
        if (p + 1) % GROUP == 0 and p + 1 < NB // 8:
            top, end = p + 1 - GROUP, p + 1
            done = jnp.concatenate(tiles[top:end], axis=0)
            row = 8 * top + lax.broadcasted_iota(jnp.int32, done.shape, 0)
            lane = lax.broadcasted_iota(jnp.int32, done.shape, 1)
            inside = (lane >= 8 * top) & (lane < 8 * end)
            later = jnp.concatenate(tiles[end:], axis=0)
            lane2 = lax.broadcasted_iota(jnp.int32, later.shape, 1)
            later = jnp.where((lane2 >= 8 * top) & (lane2 < 8 * end), 0.0, later) - exact(
                done[:, 8 * end :], jnp.where(inside & (lane > row), 0.0, done), dims(0, 0)
            )
            tiles[end:] = [later[8 * i : 8 * i + 8, :] for i in range(NB // 8 - end)]
    for i in range(NB // 8):
        z_ref[8 * i : 8 * i + 8, :] = tiles[i]


def invert_cholesky(z_ref, d_ref, between):
    lower = lax.broadcasted_iota(jnp.int32, (NB, NB), 0) >= lax.broadcasted_iota(
        jnp.int32, (NB, NB), 1
    )
    rest = []
    for b in range(R // NB):
        lo, hi = b * NB, (b + 1) * NB
        d_ref[...] = z_ref[lo:hi, lo:hi]
        invert_leaf(d_ref, lambda: between(2 * b), rest)
        while rest:
            rest.pop(0)()
        block = jnp.where(lower, d_ref[...], 0.0)
        z_ref[lo:hi, lo:hi] = block
        if hi < R:
            follow = slice(hi, hi + NB)
            first = exact(block, z_ref[lo:hi, follow], dims(1, 0))
            z_ref[follow, follow] -= exact(first, first, dims(0, 0))
            z_ref[lo:hi, follow] = first
        rest = later_work(z_ref, lo, hi, block)
        between(2 * b + 1)
    while rest:
        rest.pop(0)()
    for b in range(R // NB - 1):
        z_ref[b * NB : (b + 1) * NB, (b + 1) * NB :] = jnp.zeros((NB, R - (b + 1) * NB), F32)


def later_work(z_ref, lo, hi, block):
    parts = []
    if lo:

        def own_rows():
            z_ref[lo:hi, :lo] = exact(block, z_ref[lo:hi, :lo], dims(1, 0))

        parts.append(own_rows)
    if hi + NB < R:

        def upper_rows():
            z_ref[lo:hi, hi + NB :] = exact(block, z_ref[lo:hi, hi + NB :], dims(1, 0))

        parts.append(upper_rows)
    for i in range(hi, R, NB):
        rows = slice(i, i + NB)

        def inverse_part(rows=rows):
            zero = jnp.zeros((NB, NB), F32)
            before = jnp.concatenate([z_ref[rows, :lo], zero], axis=1) if lo else zero
            z_ref[rows, :hi] = before - exact(
                z_ref[lo:hi, rows], z_ref[lo:hi, :hi], dims(0, 0)
            )

        def upper_part(rows=rows, start=i + NB if i == hi else i):
            z_ref[rows, start:] -= exact(z_ref[lo:hi, rows], z_ref[lo:hi, start:], dims(0, 0))

        parts.append(inverse_part)
        if i + NB < R or i > hi:
            parts.append(upper_part)
    return parts


class Copies:
    def __init__(self, send_sems, recv_sems):
        self.send_sems, self.recv_sems = send_sems, recv_sems
        self.count = 0
        self.unfinished = []

    def start(self, src, dst, device):
        i = self.count
        self.count += 1
        copy = pltpu.make_async_remote_copy(
            src_ref=src,
            dst_ref=dst,
            send_sem=self.send_sems.at[i],
            recv_sem=self.recv_sems.at[i],
            device_id=device,
            device_id_type=MESH,
        )
        copy.start()
        self.unfinished.append(copy)
        return copy

    def finish(self):
        for copy in self.unfinished:
            copy.wait_send()


class Ring:
    def __init__(self, copies, place, right, left, columns=slice(None)):
        self.copies, self.place, self.right, self.left = copies, place, right, left
        self.columns = columns

    def rows(self, base, size, ahead, part=None):
        start = base + size * lax.rem(self.place + ahead, 4)
        if part is None:
            return pl.ds(pl.multiple_of(start, 8), size)
        return pl.ds(pl.multiple_of(start + part * (size // 2), 8), size // 2)

    def scatter_far(self, src, base, size, far, near):
        self.src, self.base, self.size, self.far, self.near = src, base, size, far, near
        start, cols = self.copies.start, self.columns
        self.far_right = start(
            src.at[self.rows(base, size, 2, 0), cols], far.at[0, :, cols], self.right
        )
        self.far_left = start(
            src.at[self.rows(base, size, 2, 1), cols], far.at[1, :, cols], self.left
        )

    def scatter_near(self):
        src, base, size, near, cols = self.src, self.base, self.size, self.near, self.columns
        half = size // 2
        self.near_right = self.copies.start(
            src.at[self.rows(base, size, 1, 1), cols], near.at[0, half:, cols], self.right
        )
        self.near_left = self.copies.start(
            src.at[self.rows(base, size, 3, 0), cols], near.at[1, :half, cols], self.left
        )

    def scatter_start(self, *args):
        self.scatter_far(*args)
        self.scatter_near()

    def scatter_middle(self):
        half, cols = self.size // 2, self.columns
        self.far_right.wait_recv()
        rows = self.rows(self.base, self.size, 1, 0)
        self.src[rows, cols] += self.far[0, :, cols]
        self.last_right = self.copies.start(
            self.src.at[rows, cols], self.near.at[0, :half, cols], self.right
        )
        self.far_left.wait_recv()
        rows = self.rows(self.base, self.size, 3, 1)
        self.src[rows, cols] += self.far[1, :, cols]
        self.last_left = self.copies.start(
            self.src.at[rows, cols], self.near.at[1, half:, cols], self.left
        )

    def scatter_end(self, out, out_rows):
        cols = self.columns
        for copy in (self.near_right, self.near_left, self.last_right, self.last_left):
            copy.wait_recv()
        own = self.src[self.rows(self.base, self.size, 0), cols]
        out[out_rows, cols] = own + self.near[0, :, cols] + self.near[1, :, cols]

    def gather_start(self, buf, base, size):
        self.buf, self.base, self.size = buf, base, size
        own = buf.at[self.rows(base, size, 0), self.columns]
        self.to_right = self.copies.start(own, own, self.right)
        self.to_left = self.copies.start(own, own, self.left)

    def gather_middle(self):
        self.to_right.wait_recv()
        part = self.buf.at[self.rows(self.base, self.size, 3, 0), self.columns]
        self.on_right = self.copies.start(part, part, self.right)
        self.to_left.wait_recv()
        part = self.buf.at[self.rows(self.base, self.size, 1, 1), self.columns]
        self.on_left = self.copies.start(part, part, self.left)

    def gather_end(self):
        self.on_right.wait_recv()
        self.on_left.wait_recv()


BLOCKS = [(i, j) for i in range(R // NB) for j in range(i, R // NB)]
PACKED = len(BLOCKS) * NB
LIMIT = 42 * 1024 * 1024
COPIES = 160
PIECE = PACKED // 32
CHUNKS = [slice(0, R // 2), slice(R // 2, R)]


def kernel(
    momentum, gradient, weight, basis,
    right_out, scaled_out, high_out, low_out, buffer_out, weight_out,
    mom, grad, prev, high, low, high_t, low_t,
    part, first_a, first_b, left, far_x, near_x, far_z, near_z, far_x2, near_x2, far_z2, near_z2,
    gram, packed, packed_sum, gram_in, gram_y,
    right, right_in, right_sum, right_far, right_near,
    tri, block, tri_h, tri_l, squares, square_rows,
    load_sems, send_sems, recv_sems,
):
    r, c = lax.axis_index("row"), lax.axis_index("col")
    y, core = r // 2, lax.rem(r, 2)
    z, x = c // 4, lax.rem(c, 4)

    def at(dy=0, dz=0, dx=0):
        return (
            lax.rem(y + dy, 4) * 2 + core,
            lax.rem(z + dz, 4) * 4 + lax.rem(x + dx, 4),
        )

    sibling = (y * 2 + 1 - core, c)

    order = []
    for ahead in (2, 1, 3, 0):
        order.append(lax.rem(x + ahead, 4) * SLICE)
        order.append(ROWS // 2 + lax.rem(z + ahead, 4) * SLICE)
    order = [pl.ds(pl.multiple_of(start, SLICE), SLICE) for start in order]
    load_basis = pltpu.make_async_copy(basis, prev, load_sems.at[16])
    load_basis.start()
    loads = []
    for i, rows in enumerate(order):
        a = pltpu.make_async_copy(momentum.at[rows], mom.at[rows], load_sems.at[2 * i])
        b = pltpu.make_async_copy(gradient.at[rows], grad.at[rows], load_sems.at[2 * i + 1])
        a.start()
        b.start()
        loads.append((a, b))

    barrier = pltpu.get_barrier_semaphore()
    peers = [sibling, at(dy=1), at(dy=2), at(dy=3)] + [(r, lax.rem(c + k, 16)) for k in range(1, 16)]
    for peer in peers:
        pl.semaphore_signal(barrier, inc=1, device_id=peer, device_id_type=MESH)

    copies = Copies(send_sems, recv_sems)
    x_ring = lambda cols: Ring(copies, x, at(dx=1), at(dx=3), cols)
    z_ring = lambda cols: Ring(copies, z, at(dz=1), at(dz=3), cols)
    outer = [(x_ring(cols), z_ring(cols)) for cols in CHUNKS]
    inner = [(z_ring(cols), x_ring(cols)) for cols in CHUNKS]
    rings_w = [Ring(copies, y, at(dy=1), at(dy=3), cols) for cols in CHUNKS]

    def partial_left(i):
        rows = order[i]
        for load in loads[i]:
            load.wait()
        buffer = mom[rows, :] + grad[rows, :].astype(F32)
        buffer_out[rows, :] = buffer
        h, l = split(buffer)
        high[rows, :] = h
        low[rows, :] = l
        both = dot(jnp.concatenate([h, l], axis=0), prev[...])
        part[rows, :] = both[:SLICE] + both[SLICE:]

    load_basis.wait()
    for i in range(2):
        partial_left(i)
    pl.semaphore_wait(barrier, len(peers))
    for a, b in outer:
        a.scatter_far(part, 0, SLICE, far_x, near_x)
        b.scatter_far(part, ROWS // 2, SLICE, far_z, near_z)
    for i in range(2, 6):
        partial_left(i)
    for a, b in outer:
        a.scatter_near()
        b.scatter_near()
    for i in range(6, 8):
        partial_left(i)
    for a, b in outer:
        a.scatter_middle()
        b.scatter_middle()

    load_weight = pltpu.make_async_copy(weight, weight_out, load_sems.at[17])
    load_weight.start()

    @pl.loop(0, ROWS // NB)
    def _(k):
        rows = pl.ds(pl.multiple_of(k * NB, NB), NB)
        high_t[:, rows] = high[rows, :].T
        low_t[:, rows] = low[rows, :].T

    everything = pl.ds(0, SLICE)
    for (a, b), (a2, b2) in zip(outer, inner):
        a.scatter_end(first_a, everything)
        a2.scatter_start(first_a, 0, SUB, far_z2, near_z2)
        b.scatter_end(first_b, everything)
        b2.scatter_start(first_b, 0, SUB, far_x2, near_x2)
    for a2, b2 in inner:
        a2.scatter_middle()
        b2.scatter_middle()
    base_a = x * SLICE
    base_b = ROWS // 2 + z * SLICE
    for a2, b2 in inner:
        a2.scatter_end(left, a2.rows(base_a, SUB, 0))
        a2.gather_start(left, base_a, SUB)
        b2.scatter_end(left, b2.rows(base_b, SUB, 0))
        b2.gather_start(left, base_b, SUB)
    for a2, b2 in inner:
        a2.gather_middle()
        b2.gather_middle()
    for (a, b), (a2, b2) in zip(outer, inner):
        a2.gather_end()
        a.gather_start(left, 0, SLICE)
        b2.gather_end()
        b.gather_start(left, ROWS // 2, SLICE)

    def slices(ahead):
        return (
            pl.ds(pl.multiple_of(lax.rem(x + ahead, 4) * SLICE, SLICE), SLICE),
            pl.ds(pl.multiple_of(ROWS // 2 + lax.rem(z + ahead, 4) * SLICE, SLICE), SLICE),
        )

    def halves(ahead):
        a, b = slices(ahead)
        return split(jnp.concatenate([left[a, :], left[b, :]], axis=0))

    def add_gram(ahead, first):
        h, l = halves(ahead)
        for i in range(R // NB):
            lo, hi = i * NB, (i + 1) * NB
            hl, ll = h[:, lo:hi], l[:, lo:hi]
            term = dot_t(hl, h[:, lo:]) + (
                dot_t(hl, l[:, lo:]) + dot_t(ll, h[:, lo:]) + dot_t(ll, l[:, lo:])
            )
            if first:
                gram[lo:hi, lo:] = term
            else:
                gram[lo:hi, lo:] += term

    def add_right(ahead, first, start=0, count=COLS):
        a, b = slices(ahead)
        h, l = halves(ahead)

        @pl.loop(0, count // 256)
        def _(k):
            rows = pl.ds(pl.multiple_of(start + k * 256, 256), 256)
            bh = jnp.concatenate([high_t[rows, a], high_t[rows, b]], axis=1)
            bl = jnp.concatenate([low_t[rows, a], low_t[rows, b]], axis=1)
            both = dot(jnp.concatenate([bh, bl], axis=0), h)
            term = both[:256] + (dot(bh, l) + both[256:])
            if first:
                right[rows, :] = term
            else:
                right[rows, :] += term

    add_gram(0, True)
    add_right(0, True)
    for a, b in outer:
        a.gather_middle()
        b.gather_middle()
    add_gram(1, False)
    add_gram(3, False)
    add_right(1, False)
    for a, b in outer:
        a.gather_end()
        b.gather_end()
    add_gram(2, False)

    for k, (i, j) in enumerate(BLOCKS):
        packed[k * NB : (k + 1) * NB, :] = gram[i * NB : (i + 1) * NB, j * NB : (j + 1) * NB]

    def half_of(whole, which):
        return pl.ds(pl.multiple_of(which * (whole // 2), 8), whole // 2)

    mine_g = half_of(PACKED, core)
    mine_w, other_w = half_of(COLS, core), half_of(COLS, 1 - core)

    def piece(which, of):
        return pl.ds(pl.multiple_of(which * (PACKED // 2) + of * PIECE, 8), PIECE)

    swap_g = copies.start(packed.at[piece(1 - core, c)], gram_in, sibling)
    for ahead in (3, 2):
        add_right(ahead, False, (1 - core) * (COLS // 2), COLS // 2)
    swaps_w = [
        copies.start(right.at[other_w, cols], right_in.at[:, cols], sibling)
        for cols in CHUNKS
    ]
    swap_g.wait_recv()
    gram_y[y] = packed[piece(core, c), :] + gram_in[...]
    over_y = [copies.start(gram_y.at[y], gram_y.at[y], at(dy=k)) for k in (2, 1, 3)]
    for ahead in (3, 2):
        add_right(ahead, False, core * (COLS // 2), COLS // 2)
    for cols, swap, ring in zip(CHUNKS, swaps_w, rings_w):
        swap.wait_recv()
        right[mine_w, cols] += right_in[:, cols]
        ring.scatter_far(right, core * (COLS // 2), COLS // 8, right_far, right_near)
    for copy in over_y:
        copy.wait_recv()
    own_piece = packed_sum.at[piece(core, c)]
    own_piece[...] = (gram_y[0] + gram_y[1]) + (gram_y[2] + gram_y[3])
    over_col = [
        copies.start(own_piece, own_piece, (r, lax.rem(c + k, 16))) for k in range(1, 16)
    ]
    for ring in rings_w:
        ring.scatter_near()
    for ring in rings_w:
        ring.scatter_middle()
    for copy in over_col:
        copy.wait_recv()
    back_g = copies.start(packed_sum.at[mine_g], packed_sum.at[mine_g], sibling)
    back_g.wait_recv()
    for k, (i, j) in enumerate(BLOCKS):
        tri[i * NB : (i + 1) * NB, j * NB : (j + 1) * NB] = packed_sum[k * NB : (k + 1) * NB, :]

    swaps = []

    def between(step):
        if step == 0:
            for ring in rings_w:
                ring.scatter_end(right_sum, ring.rows(core * (COLS // 2), COLS // 8, 0))
                ring.gather_start(right_sum, core * (COLS // 2), COLS // 8)
        elif step in (2, 4):
            rings_w[step // 2 - 1].gather_middle()
        elif step in (5, 6):
            ring = rings_w[step - 5]
            ring.gather_end()
            own = right_sum.at[mine_w, ring.columns]
            swaps.append(copies.start(own, own, sibling))

    invert_cholesky(tri, block, between)
    for swap in swaps:
        swap.wait_recv()

    tri_h[...], tri_l[...] = split(tri[...].T)
    square_rows[...] = jnp.zeros((8, R), F32)
    h2 = R // 2

    def solved(value):
        h, l = split(value)
        n = len(value)
        both = jnp.concatenate([h, l], axis=0)
        halves = []
        for width, out in ((h2, slice(0, h2)), (R, slice(h2, R))):
            p = dot(both[:, :width], tri_h[:width, out])
            q = dot(h[:, :width], tri_l[:width, out])
            halves.append(p[:n] + (p[n:] + q))
        return jnp.concatenate(halves, axis=1)

    @pl.loop(0, COLS // 256)
    def _(k):
        rows = pl.ds(pl.multiple_of(k * 256, 256), 256)
        value = solved(right_sum[rows, :])
        mom[rows, R:] = value
        square_rows[...] += jnp.sum((value * value).reshape(32, 8, R), axis=0)

    row = jnp.sum(square_rows[...], axis=0, keepdims=True)
    quarters = [row[:, i : i + NB] for i in range(0, R, NB)]
    squares[c] = jnp.concatenate(quarters + [jnp.zeros((4, NB), F32)], axis=0)
    sums = []
    for k in range(1, 16):
        sums.append(copies.start(squares.at[c], squares.at[c], (r, lax.rem(c + k, 16))))

    @pl.loop(0, ROWS // 256)
    def _(k):
        rows = pl.ds(pl.multiple_of(k * 256, 256), 256)
        value = solved(left[rows, :])
        mom[rows, :R] = value
        h, l = split(value)
        high_out[rows, :] = h
        low_out[rows, :] = l

    for copy in sums:
        copy.wait_recv()
    total = squares[0]
    for k in range(1, 16):
        total = total + squares[k]
    total = jnp.concatenate([total[i : i + 1, :] for i in range(R // NB)], axis=1)
    scale = jnp.sqrt(total / N + epsilon)
    inverse = 1.0 / scale
    right_out[...] = (mom[:, R:] * inverse).astype(BF16)
    scaled_out[...] = (mom[:, :R] * scale).astype(BF16)
    load_weight.wait()
    copies.finish()


def factors(momentum, gradient, weight, basis):
    vmem = pl.BlockSpec(memory_space=pltpu.VMEM)
    any_ = pl.BlockSpec(memory_space=pltpu.HBM)
    f = lambda *s: pltpu.VMEM(s, F32)
    b = lambda *s: pltpu.VMEM(s, BF16)
    ring = lambda s, w: [f(2, s // 2, w), f(2, s, w)]
    return pl.pallas_call(
        kernel,
        out_shape=[
            jax.ShapeDtypeStruct((COLS, R), BF16),
            jax.ShapeDtypeStruct((ROWS, R), BF16),
            jax.ShapeDtypeStruct((ROWS, R), BF16),
            jax.ShapeDtypeStruct((ROWS, R), BF16),
            jax.ShapeDtypeStruct((ROWS, COLS), F32),
            jax.ShapeDtypeStruct((ROWS, COLS), BF16),
        ],
        in_specs=[any_] * 4,
        out_specs=[vmem] * 6,
        scratch_shapes=[
            f(ROWS, COLS), b(ROWS, COLS), b(COLS, R),
            b(ROWS, COLS), b(ROWS, COLS), b(COLS, ROWS), b(COLS, ROWS),
            f(ROWS, R), f(SLICE, R), f(SLICE, R), f(ROWS, R),
            *ring(SLICE, R), *ring(SLICE, R), *ring(SUB, R), *ring(SUB, R),
            f(R, R), f(PACKED, NB), f(PACKED, NB), f(PIECE, NB), f(4, PIECE, NB),
            f(COLS, R), f(COLS // 2, R), f(COLS, R), *ring(COLS // 8, R),
            f(R, R), f(NB, NB), b(R, R), b(R, R), f(16, 8, NB), f(8, R),
            pltpu.SemaphoreType.DMA((18,)),
            pltpu.SemaphoreType.DMA((COPIES,)),
            pltpu.SemaphoreType.DMA((COPIES,)),
        ],
        compiler_params=pltpu.CompilerParams(
            collective_id=0, has_side_effects=True, vmem_limit_bytes=LIMIT
        ),
        name="factors",
    )(momentum, gradient, weight, basis)


def last_kernel(b, w, scaled, high, low, v, basis, new_w, new_m, new_v):
    buffer = b[...]
    vs = v[...]
    rows = len(buffer)
    both = dot_nt(jnp.concatenate([scaled[...], high[...], low[...]], axis=0), vs)
    new_m[...] = buffer - decay_loss * both[:rows]
    update = both[rows : 2 * rows] + both[2 * rows :]
    rate = step_size * (M / N) ** 0.5
    new_w[...] = (w[...].astype(F32) - rate * update).astype(BF16)
    new_v[...] = basis[...]


def outputs(buffer, weight, scaled, high, low, v):
    rows = 256
    wide = pl.BlockSpec((rows, COLS), lambda i: (i, 0))
    thin = pl.BlockSpec((rows, R), lambda i: (i, 0))
    whole = pl.BlockSpec((COLS, R), lambda i: (0, 0))
    return pl.pallas_call(
        last_kernel,
        grid=(ROWS // rows,),
        out_shape=[
            jax.ShapeDtypeStruct((ROWS, COLS), BF16),
            jax.ShapeDtypeStruct((ROWS, COLS), F32),
            jax.ShapeDtypeStruct((COLS, R), BF16),
        ],
        in_specs=[wide, wide, thin, thin, thin, whole, thin],
        out_specs=[wide, wide, thin],
        compiler_params=pltpu.CompilerParams(vmem_limit_bytes=20 * 1024 * 1024),
        name="outputs",
    )(buffer, weight, scaled, high, low, v, v)


def per_device(weight, momentum, gradient, prev_basis):
    kept = [
        pltpu.with_memory_space_constraint(a, pltpu.HBM)
        for a in (momentum, gradient, weight, prev_basis)
    ]
    v, *rest, buffer, held = factors(*kept)
    return tuple(outputs(buffer, held, *rest, v))


def solution(mesh):
    return jax.shard_map(
        per_device,
        mesh=mesh,
        in_specs=(P("row", "col"), P("row", "col"), P("row", "col"), P("col", None)),
        out_specs=(P("row", "col"), P("row", "col"), P("col", None)),
        check_vma=False,
    )
```
